32 devices in a mesh: group: 2 (over y), sky: 4 (over z), visit: 2 (over x), band: 2 (over core).
Axes of the slice: x: 2, y: 2, z: 4, core: 2. Of those that a mesh axis runs over, the one named last changes fastest.
Arguments:
- raw_tiles: bfloat16 [16, 32, 128, 128], P(('group', 'visit', 'band'), 'sky'), parts along dimension 0, may hold values from -6 to 6
- pixel_offsets: int32 [16, 32, 2], P(('group', 'visit', 'band'), 'sky'), parts along dimension 0, may hold values from -1 to 1
- shift_entry_index: int32 [16, 32], P(('group', 'visit', 'band'), 'sky'), parts along dimension 0, may hold values from 0 to 15
- shift_table: float32 [16, 2], replicated, may hold values from 0 to 1
- tile_routes: int32 [16, 32], P(('group', 'visit', 'band'), 'sky'), parts along dimension 0, may hold values from 0 to 31, as said below
- bad_pixels: int32 [16, 32, 32], P('group', 'sky'), parts along dimension 0, may hold values from 0 to 16383, as said below
- basis_kernels: bfloat16 [4, 33, 33], replicated, may hold values from -0.5 to 0.5
- basis_choice: int32 [16, 32], P(('group', 'visit', 'band'), 'sky'), parts along dimension 0, may hold values from 0 to 15
- coef_table: float32 [16, 4], replicated, may hold values from -4 to 4
Outputs:
- difference: bfloat16 [16, 512, 1024], P(('group', 'visit', 'band'), 'sky'), parts along dimension 0
The draws below stay inside these ranges and needn't reach their ends.
There are 2 independent parts, one for each index of `group`. The reference program is written for one: setup_inputs(seed, part) draws one part's arguments, and reference() takes and returns one part's arrays. A program takes and returns all parts, laid end to end along the dimension named above; an argument that names none is the same for every part. Nothing has to cross between parts.
Inputs may be any that keep to these rules, and one draw needn't show every extreme that they name: `tile_routes`: for every visit, each of the 32 slab tiles is named by exactly one source tile. Within each aligned block of 2 visits, the source tiles i with one value of i // 8 name at most 5 slab tiles t with one value of t // 8, and exactly 5 for some value. `bad_pixels`: an entry names the pixel at row r and column c of the slab tile as r * 128 + c. For one slab tile, the entries of all visits together are distinct.
All inputs are finite; a program needn't handle non-finite values.
Results may differ from the reference program's by a relative error of at most 0.018.
Values may be sent and summed in bfloat16 or wider, within the bound.
No kernel may reach another device: no remote copies, remote signals or barrier semaphores. Data moves between devices by JAX's collectives and lax.ppermute only.
A program may use at most 128 MiB of HBM per device.

```python
import jax
import jax.numpy as jnp
from jax import lax

TILE = 128
KS = 33
NB = 4
SHIFT_ENTRIES = 16
NCOEF = 16
VIS_DEV = 2
TCOLS = 8
NBAD = 32
VISITS = 8
TILES = 32
N_SKY = 4


def route_block(key):
    patches = TILES // TCOLS
    pooled_width = VIS_DEV * TCOLS
    capacity = (pooled_width + patches - 1) // patches + 1
    sub_keys = jax.random.split(key, 6)
    sigma_order = jax.random.permutation(sub_keys[0], patches).astype(jnp.int32)
    tau_order = jax.random.permutation(sub_keys[1], patches).astype(jnp.int32)
    class_offsets = jax.random.permutation(sub_keys[2], patches).astype(jnp.int32)
    slot_order = jax.random.permutation(sub_keys[3], pooled_width).astype(jnp.int32)
    seat_draw = jax.random.permutation(sub_keys[4], (patches - 1) * capacity).astype(jnp.int32)
    seat_padded = jnp.concatenate([seat_draw, jnp.zeros((pooled_width,), jnp.int32)])
    positions = jnp.zeros((pooled_width,), jnp.int32).at[slot_order].set(jnp.arange(pooled_width, dtype=jnp.int32))
    seat_index = jnp.clip(positions - capacity, 0, pooled_width - 1)
    classes = jnp.where(positions < capacity, 0, 1 + seat_padded[seat_index] // capacity)
    owners = tau_order[(sigma_order[:, None] + class_offsets[classes][None, :]) % patches]
    owner_grid = owners.reshape(patches, VIS_DEV, TCOLS).transpose(1, 0, 2)
    scores = jax.random.randint(sub_keys[5], (VIS_DEV, patches, TCOLS), 0, 1048576) * TCOLS + jnp.arange(TCOLS, dtype=jnp.int32)
    arrival = jnp.argsort(scores, axis=-1, stable=True).astype(jnp.int32)
    selected_entries = jnp.take_along_axis(arrival, owner_grid, axis=1)
    return (owner_grid * TCOLS + selected_entries).reshape(VIS_DEV, patches * TCOLS).astype(jnp.int32)


def draw_tile_routes(key, part):
    shard_keys = jax.random.split(jax.random.fold_in(key, 7), VISITS // VIS_DEV)
    return jax.vmap(route_block)(shard_keys).reshape(VISITS, TILES)


def draw_bad_pixels(key, part):
    tile_keys = jax.random.split(jax.random.fold_in(key, 11), TILES)

    def one_order(tile_key):
        return jax.random.permutation(tile_key, TILE * TILE).astype(jnp.int32)
    orders = jax.vmap(one_order)(tile_keys)
    selected_entries = orders[:, :VISITS * NBAD].reshape(TILES, VISITS, NBAD)
    return jnp.transpose(selected_entries, (1, 0, 2)).astype(jnp.int32)


def plant(entries, stream_key, low, high):
    longest = entries.shape.index(max(entries.shape))
    spots = []
    for shift in (0, 1):
        where = [jax.random.randint(jax.random.fold_in(stream_key, axis), (), 0, length) for axis, length in enumerate(entries.shape)]
        where[longest] = (where[longest] + shift) % entries.shape[longest]
        spots.append(tuple(where))
    return entries.at[spots[0]].set(low).at[spots[1]].set(high)


def levels(key, shape, pieces, low, top_value):
    factor_of = 1.0
    for dim, shards_of in pieces:
        steps = jax.random.uniform(jax.random.fold_in(jax.random.fold_in(key, 6), dim), (shards_of,), jnp.float32, low / len(pieces), top_value / len(pieces))
        factor_of = factor_of * jnp.repeat(jnp.exp(steps), shape[dim] // shards_of).reshape((-1,) + (1,) * (len(shape) - 1 - dim))
    return factor_of


def gaussian(stream_key, extent, scale, bound, shards=(), kind=jnp.bfloat16):
    level = levels(stream_key, extent, shards, -0.22, 0.18) if shards else 1.0
    result = jax.random.normal(stream_key, extent, jnp.float32) * scale * level
    return jnp.minimum(jnp.maximum(result, -bound), bound).astype(kind)


def setup_inputs(seed: int = 0, part: int = 0) -> dict:
    splits = jax.random.split(jax.random.key(seed), 10)
    part_keys = jax.random.split(jax.random.fold_in(splits[9], part), 10)
    return {
        "raw_tiles": gaussian(part_keys[0], (VISITS, TILES, TILE, TILE), 1.0, 6.0, ((0, 4), (1, 4))),
        "pixel_offsets": plant(jax.random.randint(part_keys[1], (VISITS, TILES, 2), -1, 2), jax.random.fold_in(part_keys[1], 1), -1, 1).astype(jnp.int32),
        "shift_entry_index": plant(jax.random.randint(part_keys[2], (VISITS, TILES), 0, SHIFT_ENTRIES), jax.random.fold_in(part_keys[2], 1), 0, SHIFT_ENTRIES - 1).astype(jnp.int32),
        "shift_table": jnp.clip(jax.random.uniform(splits[3], (SHIFT_ENTRIES, 2), jnp.float32, 0.0, 1.0), 0.0, 1.0),
        "tile_routes": draw_tile_routes(jax.random.fold_in(jax.random.fold_in(splits[9], part), 71), part),
        "bad_pixels": draw_bad_pixels(jax.random.fold_in(jax.random.fold_in(splits[9], part), 71), part),
        "basis_kernels": gaussian(splits[6], (NB, KS, KS), (KS * KS // 8) ** -0.5, 0.5),
        "basis_choice": plant(jax.random.randint(part_keys[7], (VISITS, TILES), 0, NCOEF), jax.random.fold_in(part_keys[7], 1), 0, NCOEF - 1).astype(jnp.int32),
        "coef_table": gaussian(splits[8], (NCOEF, NB), 1.0, 4.0, (), jnp.float32),
    }


def lanczos(offset):
    return jnp.where(jnp.abs(offset) < 3.0, jnp.sinc(offset) * jnp.sinc(offset / 3.0), 0.0)


def to_image(tiles):
    return tiles.reshape(N_SKY, TCOLS, TILE, TILE).transpose(0, 2, 1, 3).reshape(TILE * N_SKY, TCOLS * TILE)


def one_visit(raw_tile, offsets, selected_entries, routes, listed, shift_table):
    fraction = shift_table[selected_entries]
    shifts = offsets.astype(jnp.float32) + fraction
    target_positions = jnp.arange(TILE).astype(jnp.float32)
    spacing = target_positions[:, None] - target_positions[None, :]
    row_weights = lanczos(spacing[None] - shifts[:, 0, None, None]).astype(jnp.bfloat16)
    col_weights = lanczos(spacing[None] - shifts[:, 1, None, None]).astype(jnp.bfloat16)
    halfway = jnp.einsum("tap,tpq->taq", row_weights.astype(jnp.float32), raw_tile.astype(jnp.float32), precision=lax.Precision.HIGHEST).astype(jnp.bfloat16)
    warped = jnp.einsum("taq,tbq->tab", halfway.astype(jnp.float32), col_weights.astype(jnp.float32), precision=lax.Precision.HIGHEST).astype(jnp.bfloat16)
    placed = jnp.zeros_like(warped).at[routes].set(warped)
    indices = jnp.arange(TILE).astype(jnp.int32)
    row_match_count = (listed[:, None, :] // TILE == indices[None, :, None]).astype(jnp.float32)
    column_match_count = (listed[:, None, :] % TILE == indices[None, :, None]).astype(jnp.float32)
    marked_pixels = jnp.einsum("svw,srw->svr", row_match_count, column_match_count, precision=lax.Precision.HIGHEST)
    return to_image(placed), to_image(marked_pixels).astype(jnp.bfloat16)


def reference(raw_tiles, pixel_offsets, shift_entry_index, shift_table, tile_routes, bad_pixels, basis_kernels, basis_choice, coef_table):
    def visit_step(inputs):
        raw_tile, offsets, selected_entries, routes, listed = inputs
        return one_visit(raw_tile, offsets, selected_entries, routes, listed, shift_table)

    slab_images, marked_pixels = lax.map(visit_step, (raw_tiles, pixel_offsets, shift_entry_index, tile_routes, bad_pixels))
    valid_pixel_mask = 1.0 - marked_pixels.astype(jnp.float32)
    values = slab_images.astype(jnp.float32)
    summed = jnp.sum(valid_pixel_mask * values, axis=0)
    tallies = jnp.sum(valid_pixel_mask, axis=0)
    highest = jnp.max(jnp.where(valid_pixel_mask > 0.5, values, -jnp.inf), axis=0)
    lowest = jnp.min(jnp.where(valid_pixel_mask > 0.5, values, jnp.inf), axis=0)
    coadded = ((summed - highest - lowest) / (tallies - 2.0)).astype(jnp.bfloat16)
    margin = KS // 2
    filtered = lax.conv_general_dilated(coadded.astype(jnp.float32)[None, None], basis_kernels.astype(jnp.float32)[:, None], (1, 1), ((margin, margin), (margin, margin)), precision=lax.Precision.HIGHEST)[0].astype(jnp.bfloat16)
    mixture = coef_table[basis_choice].reshape(VISITS, N_SKY, TCOLS, NB)
    basis_planes = filtered.astype(jnp.float32).reshape(NB, N_SKY, TILE, TCOLS, TILE)
    template = jnp.einsum("vskb,bsakc->vsakc", mixture, basis_planes, precision=lax.Precision.HIGHEST).reshape(VISITS, TILE * N_SKY, TCOLS * TILE)
    return ((values - template) * valid_pixel_mask).astype(jnp.bfloat16)
```

```python
import functools

import jax
import jax.numpy as jnp
from jax import lax
from jax.experimental import pallas as pl
from jax.experimental.pallas import tpu as pltpu
from jax.sharding import PartitionSpec as P

BF = jnp.bfloat16
F32 = jnp.float32
I32 = jnp.int32
VMEM = pl.BlockSpec(memory_space=pltpu.VMEM)
SMEM = pl.BlockSpec(memory_space=pltpu.SMEM)
LABELS = 8


def kernel_call(body, outs, in_specs, scratch=(), flops=0, data=0, name=None):
    return pl.pallas_call(
        body,
        out_shape=outs,
        in_specs=in_specs,
        out_specs=jax.tree.map(lambda _: VMEM, outs),
        scratch_shapes=list(scratch),
        cost_estimate=pl.CostEstimate(flops=flops, bytes_accessed=data, transcendentals=0),
        name=name,
    )


def sinc(x):
    angle = x * jnp.float32(jnp.pi)
    safe = jnp.where(x == 0.0, 1.0, angle)
    return jnp.where(x == 0.0, 1.0, jnp.sin(safe) / safe)


def iota(shape, dim):
    return lax.broadcasted_iota(I32, shape, dim)


def warp_body(patches, visits, cap, routes, offsets, entries, table, raw, *refs):
    parcels, (seats, labels, count) = refs[:-3], refs[-3:]
    visit_count, tile_cols, side, _ = raw.shape
    tiles = visit_count * tile_cols
    part = side // visits
    sky, visit = lax.axis_index("sky"), lax.axis_index("visit")
    row = iota((2 * tiles, side), 0)
    shift = jnp.zeros((2 * tiles, side), F32)
    for n in range(tiles):
        v, i = divmod(n, tile_cols)
        entry = entries[v, i]
        for axis in range(2):
            amount = offsets[v, i, axis].astype(F32) + table[entry, axis]
            shift = jnp.where(row == 2 * n + axis, amount, shift)
    lane = iota((2 * tiles, side), 1)
    step = jnp.where(lane < side // 2, lane, lane - side)
    x = jnp.where(row % 2 == 0, -step, step).astype(F32) - shift
    taps = jnp.where(jnp.abs(x) < 3.0, sinc(x) * sinc(x / 3.0), 0.0)
    near = jnp.abs(iota((side, side), 1) - iota((side, side), 0)) < side // 2

    def spread(index):
        rows = jnp.broadcast_to(taps[index : index + 1, :], (side, side))
        rolled = pltpu.roll(rows, 0, 1, stride=1, stride_axis=0)
        return jnp.where(near, rolled, 0.0).astype(BF)

    for k in range(patches):
        count[k] = 0
        labels[k] = jnp.full((LABELS, side), -1.0, F32)
    for n in range(tiles):
        v, i = divmod(n, tile_cols)
        halfway = jnp.dot(spread(2 * n), raw[v, i], preferred_element_type=F32).astype(BF)
        warped = jnp.dot(halfway, spread(2 * n + 1), preferred_element_type=F32).astype(BF)
        route = routes[v, i]
        owner = lax.div(route, tile_cols)
        slot = route - owner * tile_cols
        relative = lax.rem(owner - sky + patches, patches)
        seat = count[relative]
        count[relative] = seat + 1
        seats[relative * cap + seat] = warped
        labels[relative, pl.ds(seat, 1), :] = jnp.full(
            (1, side), ((visit * visit_count + v) * tile_cols + slot).astype(F32), F32
        )
    for k in range(patches):
        for r in range(visits):
            parcel = parcels[k * visits + r]
            target = lax.rem(visit + r, visits)
            rows = pl.ds(pl.multiple_of(target * part, part), part)
            for seat in range(cap):
                parcel[seat * part : (seat + 1) * part, :] = seats[k * cap + seat, rows, :]
            parcel[cap * part :, :] = labels[k].astype(BF)


def warp_tiles(patches, visits, cap, raw, offsets, entries, table, routes):
    visit_count, tile_cols, side, _ = raw.shape
    parcel = jax.ShapeDtypeStruct((cap * (side // visits) + LABELS, side), BF)
    return kernel_call(
        functools.partial(warp_body, patches, visits, cap),
        [parcel] * (patches * visits),
        [SMEM] * 4 + [VMEM],
        [
            pltpu.VMEM((patches * cap, side, side), BF),
            pltpu.VMEM((patches, LABELS, side), F32),
            pltpu.SMEM((patches,), I32),
        ],
        flops=4 * visit_count * tile_cols * side**3,
        data=4 * raw.size,
        name="warp",
    )(routes, offsets, entries, table, raw)


def tables_body(side, block, listed, taps, plane, bands):
    visit_total, tile_cols, per = listed.shape
    width = visit_total * per
    bad = jnp.concatenate([listed[v] for v in range(visit_total)], axis=1)
    bad_row = lax.div(bad, side)
    bad_col = bad - bad_row * side
    place = iota((side, width), 0)
    weight = (lax.div(iota((side, width), 1), per) + 1).astype(F32)
    for t in range(tile_cols):
        rows = jnp.where(bad_row[t : t + 1, :] == place, 1.0, 0.0).astype(BF)
        cols = jnp.where(bad_col[t : t + 1, :] == place, weight, 0.0).astype(BF)
        plane[:, t * side : (t + 1) * side] = lax.dot_general(
            rows, cols, (((1,), (1,)), ((), ())), preferred_element_type=F32
        )
    bases, pairs, lanes = taps.shape
    for b in range(bases):
        for j in range(pairs):
            rows = jnp.broadcast_to(taps[b, j : j + 1, :], (block, lanes))
            bands[b * block : (b + 1) * block, j * lanes : (j + 1) * lanes] = pltpu.roll(
                rows, 0, 1, stride=1, stride_axis=0
            ).astype(BF)


def make_tables(listed, kernels, side, block):
    visit_total, tile_cols, per = listed.shape
    bases, taps, _ = kernels.shape
    window = block + taps - 1
    group = max(1, 128 // window)
    padded = -(-taps // group) * group
    columns = jnp.pad(
        jnp.transpose(kernels, (0, 2, 1)).astype(F32), ((0, 0), (0, padded - taps), (0, window - taps))
    ).reshape(bases, padded // group, group * window)
    return kernel_call(
        functools.partial(tables_body, side, block),
        [
            jax.ShapeDtypeStruct((side, tile_cols * side), F32),
            jax.ShapeDtypeStruct((bases * block, padded * window), BF),
        ],
        [VMEM] * 2,
        flops=2 * tile_cols * side * side * visit_total * per,
        data=4 * side * side * tile_cols,
        name="tables",
    )(listed, columns)


def land_body(visits, bands, visit_count, cap, plane, *refs):
    count = len(refs) - 2 - visits
    parcels, slabs, partial, image = refs[:count], refs[count:-2], refs[-2], refs[-1]
    side = parcels[0].shape[1]
    part = (parcels[0].shape[0] - LABELS) // cap
    tile_cols = image.shape[2] // side
    held = visits * visit_count
    visit, band = lax.axis_index("visit"), lax.axis_index("band")
    for parcel in parcels:
        labels = parcel[cap * part :, :].astype(F32)
        for seat in range(cap):
            label = labels[seat, 0].astype(I32)
            label = jnp.where(label < 0, held * tile_cols, label)
            which = lax.div(label, tile_cols)
            column = (label - which * tile_cols) * side
            image[which, :, pl.ds(pl.multiple_of(column, side), side)] = parcel[
                seat * part : (seat + 1) * part, :
            ]
    mine = plane[pl.ds(pl.multiple_of(visit * part, part), part), :]
    total = jnp.zeros(mine.shape, F32)
    high = jnp.full(mine.shape, -jnp.inf, F32)
    low = jnp.full(mine.shape, jnp.inf, F32)
    for n in range(held):
        own, local = divmod(n, visit_count)
        number = ((own * bands + band) * visit_count + local + 1).astype(F32)
        value = image[n].astype(F32)
        bad = mine == number
        total = total + jnp.where(bad, 0.0, value)
        high = jnp.maximum(high, jnp.where(bad, -jnp.inf, value))
        low = jnp.minimum(low, jnp.where(bad, jnp.inf, value))
    partial[0] = total.astype(BF)
    partial[1] = high.astype(BF)
    partial[2] = low.astype(BF)
    for r in range(visits):
        base = lax.rem(visit + r, visits) * visit_count
        for j in range(visit_count):
            slabs[r][j] = image[base + j]


def land_tiles(visits, bands, visit_count, cap, tile_cols, plane, parcels):
    side = parcels[0].shape[1]
    part = (parcels[0].shape[0] - LABELS) // cap
    width = tile_cols * side
    out = kernel_call(
        functools.partial(land_body, visits, bands, visit_count, cap),
        [jax.ShapeDtypeStruct((visit_count, part, width), BF)] * visits
        + [jax.ShapeDtypeStruct((3, part, width), BF)],
        [VMEM] * (1 + len(parcels)),
        [pltpu.VMEM((visits * visit_count + 1, part, width), BF)],
        flops=10 * visits * visit_count * part * width,
        data=4 * visits * visit_count * part * width,
        name="land",
    )(plane, *parcels)
    return out[:-1], out[-1]


def coadd_body(visit_total, margin, plane, *refs):
    partials, (coadd, edge) = refs[:-2], refs[-2:]
    part = coadd.shape[0]
    visit = lax.axis_index("visit")
    mine = plane[pl.ds(pl.multiple_of(visit * part, part), part), :]
    total, high, low = (partials[0][n].astype(F32) for n in range(3))
    for other in partials[1:]:
        total = total + other[0].astype(F32)
        high = jnp.maximum(high, other[1].astype(F32))
        low = jnp.minimum(low, other[2].astype(F32))
    scale = jnp.where(mine > 0.0, 1.0 / (visit_total - 3.0), 1.0 / (visit_total - 2.0))
    coadd[...] = ((total - high - low) * scale).astype(BF)
    start = pl.multiple_of(jnp.where(visit == 0, 0, part - margin), margin)
    edge[...] = coadd[pl.ds(start, margin), :]


def filter_body(visits, margin, bands, *refs):
    pieces, halos = refs[:visits], refs[visits : 2 * visits]
    out, image, moved = refs[2 * visits :]
    visit = lax.axis_index("visit")
    part, width = pieces[0].shape
    taps = moved.shape[0]
    above, below = halos[0][...], halos[0][...]
    for r in range(visits):
        below = jnp.where(visit == r, halos[r][...], below)
        above = jnp.where(visits - 1 - visit == r, halos[r][...], above)
    image[:margin, :] = above.astype(F32)
    image[margin + visits * part :, :] = below.astype(F32)
    for r in range(visits):
        start = pl.multiple_of(lax.rem(visit + r, visits) * part + margin, margin)
        image[pl.ds(start, part), :] = pieces[r][...].astype(F32)
    column = iota((image.shape[0], width), 1)
    for dx in range(taps):
        rolled = pltpu.roll(image[...], (margin - dx) % width, 1)
        if dx < margin:
            rolled = jnp.where(column >= margin - dx, rolled, 0.0)
        elif dx > margin:
            rolled = jnp.where(column < width + margin - dx, rolled, 0.0)
        moved[dx] = rolled.astype(BF)
    blocks = out.shape[0]
    block = visits * part // blocks
    window = block + 2 * margin
    step = min(256, width)
    left = bands[:, : taps * window]
    for n in range(blocks):
        for c in range(0, width, step):
            right = moved[:, n * block : n * block + window, c : c + step].reshape(taps * window, step)
            out[n, :, c : c + step] = jnp.dot(left, right, preferred_element_type=F32).astype(BF)


def finish_body(visits, bands, choice, coefs, filtered, plane, *refs):
    slabs, out, image = refs[:visits], refs[-2], refs[-1]
    visit, band = lax.axis_index("visit"), lax.axis_index("band")
    visit_count, part, width = slabs[0].shape
    blocks = filtered.shape[0]
    bases = coefs.shape[1]
    block = filtered.shape[1] // bases
    tile_cols = choice.shape[1]
    side = width // tile_cols
    for r in range(visits):
        start = pl.multiple_of(lax.rem(visit + r, visits) * part, part)
        image[:, pl.ds(start, part), :] = slabs[r][...]
    for t in range(tile_cols):
        cols = slice(t * side, (t + 1) * side)
        mixture = [
            [coefs[choice[j, t], b] for b in range(bases)] for j in range(visit_count)
        ]
        for n in range(blocks):
            rows = slice(n * block, (n + 1) * block)
            planes = [
                filtered[n, b * block : (b + 1) * block, cols].astype(F32) for b in range(bases)
            ]
            bad = plane[rows, cols]
            for j in range(visit_count):
                template = sum(m * p for m, p in zip(mixture[j], planes))
                number = ((visit * bands + band) * visit_count + j + 1).astype(F32)
                value = image[j, rows, cols].astype(F32) - template
                out[j, rows, cols] = jnp.where(bad == number, 0.0, value).astype(BF)


def on_device(
    raw_tiles,
    pixel_offsets,
    shift_entry_index,
    shift_table,
    tile_routes,
    bad_pixels,
    basis_kernels,
    basis_choice,
    coef_table,
):
    visit_count, tile_cols, side = raw_tiles.shape[:3]
    patches, visits, bands = (lax.axis_size(name) for name in ("sky", "visit", "band"))
    cap = (visit_count * tile_cols + patches - 1) // patches + 1
    part, width = side // visits, tile_cols * side
    visit_total = bad_pixels.shape[0]
    bases, taps = basis_kernels.shape[:2]
    margin = taps // 2
    block = 2 * margin

    parcels = warp_tiles(
        patches, visits, cap, raw_tiles, pixel_offsets, shift_entry_index, shift_table, tile_routes
    )
    order = sorted(
        range(1, patches * visits), key=lambda n: -min(n // visits, patches - n // visits)
    )
    arrived = [parcels[0]]
    for n in order:
        k, r = divmod(n, visits)
        pairs = [
            (s * visits + v, (s + k) % patches * visits + (v + r) % visits)
            for s in range(patches)
            for v in range(visits)
        ]
        arrived.append(lax.ppermute(parcels[n], ("sky", "visit"), pairs))
    plane, toeplitz = make_tables(bad_pixels, basis_kernels, side, block)
    slabs, partial = land_tiles(visits, bands, visit_count, cap, tile_cols, plane, arrived)

    partials = [partial] + [
        lax.ppermute(partial, "band", [(b, (b + q) % bands) for b in range(bands)])
        for q in range(1, bands)
    ]
    coadd, edge = kernel_call(
        functools.partial(coadd_body, visit_total, margin),
        [jax.ShapeDtypeStruct((part, width), BF), jax.ShapeDtypeStruct((margin, width), BF)],
        [VMEM] * (1 + bands),
        flops=8 * part * width,
        data=8 * part * width,
        name="coadd",
    )(plane, *partials)

    def turn(r):
        return [(v, (v - r) % visits) for v in range(visits)]

    pieces = [coadd] + [lax.ppermute(coadd, "visit", turn(r)) for r in range(1, visits)]
    halos = []
    for r in range(visits):
        top = [(s * visits, (s - 1) * visits + r) for s in range(1, patches)]
        bottom = [
            (s * visits + visits - 1, (s + 1) * visits + visits - 1 - r) for s in range(patches - 1)
        ]
        halos.append(lax.ppermute(edge, ("sky", "visit"), top + bottom))
    own = [slabs[0]] + [
        lax.ppermute(slabs[r], "visit", [(v, (v + r) % visits) for v in range(visits)])
        for r in range(1, visits)
    ]
    own = [own[0]] + [own[visits - r] for r in range(1, visits)]
    filtered = kernel_call(
        functools.partial(filter_body, visits, margin),
        jax.ShapeDtypeStruct((side // block, bases * block, width), BF),
        [VMEM] * (1 + 2 * visits),
        [
            pltpu.VMEM((side + 2 * margin, width), F32),
            pltpu.VMEM((taps, side + 2 * margin, width), BF),
        ],
        flops=2 * bases * side * width * taps * (block + taps - 1),
        data=2 * bases * side * width,
        name="filter",
    )(toeplitz, *pieces, *halos)
    return kernel_call(
        functools.partial(finish_body, visits, bands),
        jax.ShapeDtypeStruct((visit_count, side, width), BF),
        [SMEM] * 2 + [VMEM] * (2 + visits),
        [pltpu.VMEM((visit_count, side, width), BF)],
        flops=20 * visit_count * side * width,
        data=4 * visit_count * side * width,
        name="finish",
    )(basis_choice, coef_table, filtered, plane, *own)


def solution(mesh):
    return jax.shard_map(
        on_device,
        mesh=mesh,
        in_specs=(
            P(("group", "visit", "band"), "sky", None, None),
            P(("group", "visit", "band"), "sky", None),
            P(("group", "visit", "band"), "sky"),
            P(),
            P(("group", "visit", "band"), "sky"),
            P("group", "sky", None),
            P(),
            P(("group", "visit", "band"), "sky"),
            P(),
        ),
        out_specs=P(("group", "visit", "band"), "sky", None),
        check_vma=False,
    )
```

```python
import functools
import math

import jax
import jax.numpy as jnp
from jax import lax
from jax.experimental import pallas as pl
from jax.experimental.pallas import tpu as pltpu
from jax.sharding import PartitionSpec as P

BF = jnp.bfloat16
F32 = jnp.float32
I32 = jnp.int32
VMEM = pl.BlockSpec(memory_space=pltpu.VMEM)
SMEM = pl.BlockSpec(memory_space=pltpu.SMEM)
LABELS = 8


def kernel_call(body, outs, in_specs, scratch=(), flops=0, data=0, name=None):
    def call(*args):
        held = [*args, *jax.tree.leaves(outs), *(s for s in scratch if len(s.shape) > 1)]
        room = sum(math.prod(a.shape) * jnp.dtype(a.dtype).itemsize for a in held)
        return pl.pallas_call(
            body,
            out_shape=outs,
            in_specs=in_specs,
            out_specs=jax.tree.map(lambda _: VMEM, outs),
            scratch_shapes=list(scratch),
            cost_estimate=pl.CostEstimate(flops=flops, bytes_accessed=data, transcendentals=0),
            compiler_params=pltpu.CompilerParams(vmem_limit_bytes=room + room // 4 + (4 << 20)),
            name=name,
        )(*args)

    return call


def sinc(x):
    angle = x * jnp.float32(jnp.pi)
    safe = jnp.where(x == 0.0, 1.0, angle)
    return jnp.where(x == 0.0, 1.0, jnp.sin(safe) / safe)


def iota(shape, dim):
    return lax.broadcasted_iota(I32, shape, dim)


def warp_body(patches, visits, cap, routes, offsets, entries, table, raw, *refs):
    parcels, (seats, labels, count) = refs[:-3], refs[-3:]
    visit_count, tile_cols, side, _ = raw.shape
    tiles = visit_count * tile_cols
    part = side // visits
    sky, visit = lax.axis_index("sky"), lax.axis_index("visit")
    row = iota((2 * tiles, side), 0)
    shift = jnp.zeros((2 * tiles, side), F32)
    for n in range(tiles):
        v, i = divmod(n, tile_cols)
        entry = entries[v, i]
        for axis in range(2):
            amount = offsets[v, axis, i].astype(F32) + table[axis, entry]
            shift = jnp.where(row == 2 * n + axis, amount, shift)
    lane = iota((2 * tiles, side), 1)
    step = jnp.where(lane < side // 2, lane, lane - side)
    x = jnp.where(row % 2 == 0, -step, step).astype(F32) - shift
    taps = jnp.where(jnp.abs(x) < 3.0, sinc(x) * sinc(x / 3.0), 0.0)
    near = jnp.abs(iota((side, side), 1) - iota((side, side), 0)) < side // 2

    def spread(index):
        rows = jnp.broadcast_to(taps[index : index + 1, :], (side, side))
        rolled = pltpu.roll(rows, 0, 1, stride=1, stride_axis=0)
        return jnp.where(near, rolled, 0.0).astype(BF)

    for k in range(patches):
        count[k] = 0
        labels[k] = jnp.full((LABELS, side), -1.0, F32)
    for n in range(tiles):
        v, i = divmod(n, tile_cols)
        halfway = jnp.dot(spread(2 * n), raw[v, i], preferred_element_type=F32).astype(BF)
        warped = jnp.dot(halfway, spread(2 * n + 1), preferred_element_type=F32).astype(BF)
        route = routes[v, i]
        owner = lax.div(route, tile_cols)
        slot = route - owner * tile_cols
        relative = lax.rem(owner - sky + patches, patches)
        seat = count[relative]
        count[relative] = seat + 1
        seats[relative * cap + seat] = warped
        labels[relative, pl.ds(seat, 1), :] = jnp.full(
            (1, side), ((visit * visit_count + v) * tile_cols + slot).astype(F32), F32
        )
    for k in range(patches):
        for r in range(visits):
            parcel = parcels[k * visits + r]
            target = lax.rem(visit + r, visits)
            rows = pl.ds(pl.multiple_of(target * part, part), part)
            for seat in range(cap):
                parcel[seat * part : (seat + 1) * part, :] = seats[k * cap + seat, rows, :]
            parcel[cap * part :, :] = labels[k].astype(BF)


def warp_tiles(patches, visits, cap, raw, offsets, entries, table, routes):
    visit_count, tile_cols, side, _ = raw.shape
    parcel = jax.ShapeDtypeStruct((cap * (side // visits) + LABELS, side), BF)
    return kernel_call(
        functools.partial(warp_body, patches, visits, cap),
        [parcel] * (patches * visits),
        [SMEM] * 4 + [VMEM],
        [
            pltpu.VMEM((patches * cap, side, side), BF),
            pltpu.VMEM((patches, LABELS, side), F32),
            pltpu.SMEM((patches,), I32),
        ],
        flops=4 * visit_count * tile_cols * side**3,
        data=4 * raw.size,
        name="warp",
    )(routes, jnp.transpose(offsets, (0, 2, 1)), entries, table.T, raw)


def tables_body(side, block, listed, taps, plane, bands):
    visit_total, tile_cols, per = listed.shape
    width = visit_total * per
    bad = jnp.concatenate([listed[v] for v in range(visit_total)], axis=1)
    bad_row = lax.div(bad, side)
    bad_col = bad - bad_row * side
    place = iota((side, width), 0)
    weight = (lax.div(iota((side, width), 1), per) + 1).astype(F32)
    for t in range(tile_cols):
        rows = jnp.where(bad_row[t : t + 1, :] == place, 1.0, 0.0).astype(BF)
        cols = jnp.where(bad_col[t : t + 1, :] == place, weight, 0.0).astype(BF)
        plane[:, t * side : (t + 1) * side] = lax.dot_general(
            rows, cols, (((1,), (1,)), ((), ())), preferred_element_type=F32
        )
    bases, pairs, lanes = taps.shape
    for b in range(bases):
        for j in range(pairs):
            rows = jnp.broadcast_to(taps[b, j : j + 1, :], (block, lanes))
            bands[b * block : (b + 1) * block, j * lanes : (j + 1) * lanes] = pltpu.roll(
                rows, 0, 1, stride=1, stride_axis=0
            ).astype(BF)


def make_tables(listed, kernels, side, block):
    visit_total, tile_cols, per = listed.shape
    bases, taps, _ = kernels.shape
    window = block + taps - 1
    group = max(1, 128 // window)
    padded = -(-taps // group) * group
    columns = jnp.pad(
        jnp.transpose(kernels, (0, 2, 1)).astype(F32), ((0, 0), (0, padded - taps), (0, window - taps))
    ).reshape(bases, padded // group, group * window)
    return kernel_call(
        functools.partial(tables_body, side, block),
        [
            jax.ShapeDtypeStruct((side, tile_cols * side), F32),
            jax.ShapeDtypeStruct((bases * block, padded * window), BF),
        ],
        [VMEM] * 2,
        flops=2 * tile_cols * side * side * visit_total * per,
        data=4 * side * side * tile_cols,
        name="tables",
    )(listed, columns)


def land_body(visits, bands, visit_count, cap, plane, *refs):
    count = len(refs) - 2 - visits
    parcels, slabs, partial, image = refs[:count], refs[count:-2], refs[-2], refs[-1]
    side = parcels[0].shape[1]
    part = (parcels[0].shape[0] - LABELS) // cap
    tile_cols = image.shape[2] // side
    held = visits * visit_count
    visit, band = lax.axis_index("visit"), lax.axis_index("band")
    for parcel in parcels:
        labels = parcel[cap * part :, :].astype(F32)
        for seat in range(cap):
            label = labels[seat, 0].astype(I32)
            label = jnp.where(label < 0, held * tile_cols, label)
            which = lax.div(label, tile_cols)
            column = (label - which * tile_cols) * side
            image[which, :, pl.ds(pl.multiple_of(column, side), side)] = parcel[
                seat * part : (seat + 1) * part, :
            ]
    mine = plane[pl.ds(pl.multiple_of(visit * part, part), part), :]
    total = jnp.zeros(mine.shape, F32)
    high = jnp.full(mine.shape, -jnp.inf, F32)
    low = jnp.full(mine.shape, jnp.inf, F32)
    for n in range(held):
        own, local = divmod(n, visit_count)
        number = ((own * bands + band) * visit_count + local + 1).astype(F32)
        value = image[n].astype(F32)
        bad = mine == number
        total = total + jnp.where(bad, 0.0, value)
        high = jnp.maximum(high, jnp.where(bad, -jnp.inf, value))
        low = jnp.minimum(low, jnp.where(bad, jnp.inf, value))
    partial[0] = total.astype(BF)
    partial[1] = high.astype(BF)
    partial[2] = low.astype(BF)
    for r in range(visits):
        base = lax.rem(visit + r, visits) * visit_count
        for j in range(visit_count):
            slabs[r][j] = image[base + j]


def land_tiles(visits, bands, visit_count, cap, tile_cols, plane, parcels):
    side = parcels[0].shape[1]
    part = (parcels[0].shape[0] - LABELS) // cap
    width = tile_cols * side
    out = kernel_call(
        functools.partial(land_body, visits, bands, visit_count, cap),
        [jax.ShapeDtypeStruct((visit_count, part, width), BF)] * visits
        + [jax.ShapeDtypeStruct((3, part, width), BF)],
        [VMEM] * (1 + len(parcels)),
        [pltpu.VMEM((visits * visit_count + 1, part, width), BF)],
        flops=10 * visits * visit_count * part * width,
        data=4 * visits * visit_count * part * width,
        name="land",
    )(plane, *parcels)
    return out[:-1], out[-1]


def coadd_body(visit_total, margin, plane, *refs):
    partials, (coadd, edge) = refs[:-2], refs[-2:]
    part = coadd.shape[0]
    visit = lax.axis_index("visit")
    mine = plane[pl.ds(pl.multiple_of(visit * part, part), part), :]
    total, high, low = (partials[0][n].astype(F32) for n in range(3))
    for other in partials[1:]:
        total = total + other[0].astype(F32)
        high = jnp.maximum(high, other[1].astype(F32))
        low = jnp.minimum(low, other[2].astype(F32))
    scale = jnp.where(mine > 0.0, 1.0 / (visit_total - 3.0), 1.0 / (visit_total - 2.0))
    coadd[...] = ((total - high - low) * scale).astype(BF)
    start = pl.multiple_of(jnp.where(visit == 0, 0, part - margin), margin)
    edge[...] = coadd[pl.ds(start, margin), :]


def filter_body(visits, margin, bands, *refs):
    pieces, halos = refs[:visits], refs[visits : 2 * visits]
    out, image, moved = refs[2 * visits :]
    visit = lax.axis_index("visit")
    part, width = pieces[0].shape
    taps = moved.shape[0]
    above, below = halos[0][...], halos[0][...]
    for r in range(visits):
        below = jnp.where(visit == r, halos[r][...], below)
        above = jnp.where(visits - 1 - visit == r, halos[r][...], above)
    image[:margin, :] = above.astype(F32)
    image[margin + visits * part :, :] = below.astype(F32)
    for r in range(visits):
        start = pl.multiple_of(lax.rem(visit + r, visits) * part + margin, margin)
        image[pl.ds(start, part), :] = pieces[r][...].astype(F32)
    column = iota((image.shape[0], width), 1)
    for dx in range(taps):
        rolled = pltpu.roll(image[...], (margin - dx) % width, 1)
        if dx < margin:
            rolled = jnp.where(column >= margin - dx, rolled, 0.0)
        elif dx > margin:
            rolled = jnp.where(column < width + margin - dx, rolled, 0.0)
        moved[dx] = rolled.astype(BF)
    blocks = out.shape[0]
    block = visits * part // blocks
    window = block + 2 * margin
    step = min(256, width)
    left = bands[:, : taps * window]
    for n in range(blocks):
        for c in range(0, width, step):
            right = moved[:, n * block : n * block + window, c : c + step].reshape(taps * window, step)
            out[n, :, c : c + step] = jnp.dot(left, right, preferred_element_type=F32).astype(BF)


def finish_body(visits, bands, choice, coefs, filtered, plane, *refs):
    slabs, out, image = refs[:visits], refs[-2], refs[-1]
    visit, band = lax.axis_index("visit"), lax.axis_index("band")
    visit_count, part, width = slabs[0].shape
    blocks = filtered.shape[0]
    bases = coefs.shape[0]
    block = filtered.shape[1] // bases
    tile_cols = choice.shape[1]
    side = width // tile_cols
    for r in range(visits):
        start = pl.multiple_of(lax.rem(visit + r, visits) * part, part)
        image[:, pl.ds(start, part), :] = slabs[r][...]
    for t in range(tile_cols):
        cols = slice(t * side, (t + 1) * side)
        mixture = [
            [coefs[b, choice[j, t]] for b in range(bases)] for j in range(visit_count)
        ]
        for n in range(blocks):
            rows = slice(n * block, (n + 1) * block)
            planes = [
                filtered[n, b * block : (b + 1) * block, cols].astype(F32) for b in range(bases)
            ]
            bad = plane[rows, cols]
            for j in range(visit_count):
                template = sum(m * p for m, p in zip(mixture[j], planes))
                number = ((visit * bands + band) * visit_count + j + 1).astype(F32)
                value = image[j, rows, cols].astype(F32) - template
                out[j, rows, cols] = jnp.where(bad == number, 0.0, value).astype(BF)


def on_device(
    raw_tiles,
    pixel_offsets,
    shift_entry_index,
    shift_table,
    tile_routes,
    bad_pixels,
    basis_kernels,
    basis_choice,
    coef_table,
):
    visit_count, tile_cols, side = raw_tiles.shape[:3]
    patches, visits, bands = (lax.axis_size(name) for name in ("sky", "visit", "band"))
    cap = (visit_count * tile_cols + patches - 1) // patches + 1
    part, width = side // visits, tile_cols * side
    visit_total = bad_pixels.shape[0]
    bases, taps = basis_kernels.shape[:2]
    margin = taps // 2
    block = 2 * margin

    parcels = warp_tiles(
        patches, visits, cap, raw_tiles, pixel_offsets, shift_entry_index, shift_table, tile_routes
    )
    order = sorted(
        range(1, patches * visits), key=lambda n: -min(n // visits, patches - n // visits)
    )
    arrived = [parcels[0]]
    for n in order:
        k, r = divmod(n, visits)
        pairs = [
            (s * visits + v, (s + k) % patches * visits + (v + r) % visits)
            for s in range(patches)
            for v in range(visits)
        ]
        arrived.append(lax.ppermute(parcels[n], ("sky", "visit"), pairs))
    plane, toeplitz = make_tables(bad_pixels, basis_kernels, side, block)
    slabs, partial = land_tiles(visits, bands, visit_count, cap, tile_cols, plane, arrived)

    partials = [partial] + [
        lax.ppermute(partial, "band", [(b, (b + q) % bands) for b in range(bands)])
        for q in range(1, bands)
    ]
    coadd, edge = kernel_call(
        functools.partial(coadd_body, visit_total, margin),
        [jax.ShapeDtypeStruct((part, width), BF), jax.ShapeDtypeStruct((margin, width), BF)],
        [VMEM] * (1 + bands),
        flops=8 * part * width,
        data=8 * part * width,
        name="coadd",
    )(plane, *partials)

    def turn(r):
        return [(v, (v - r) % visits) for v in range(visits)]

    pieces = [coadd] + [lax.ppermute(coadd, "visit", turn(r)) for r in range(1, visits)]
    halos = []
    for r in range(visits):
        top = [(s * visits, (s - 1) * visits + r) for s in range(1, patches)]
        bottom = [
            (s * visits + visits - 1, (s + 1) * visits + visits - 1 - r) for s in range(patches - 1)
        ]
        halos.append(lax.ppermute(edge, ("sky", "visit"), top + bottom))
    pieces, halos, slabs = lax.optimization_barrier((pieces, halos, slabs))
    own = [slabs[0]] + [
        lax.ppermute(slabs[r], "visit", [(v, (v + r) % visits) for v in range(visits)])
        for r in range(1, visits)
    ]
    own = [own[0]] + [own[visits - r] for r in range(1, visits)]
    filtered = kernel_call(
        functools.partial(filter_body, visits, margin),
        jax.ShapeDtypeStruct((side // block, bases * block, width), BF),
        [VMEM] * (1 + 2 * visits),
        [
            pltpu.VMEM((side + 2 * margin, width), F32),
            pltpu.VMEM((taps, side + 2 * margin, width), BF),
        ],
        flops=2 * bases * side * width * taps * (block + taps - 1),
        data=2 * bases * side * width,
        name="filter",
    )(toeplitz, *pieces, *halos)
    return kernel_call(
        functools.partial(finish_body, visits, bands),
        jax.ShapeDtypeStruct((visit_count, side, width), BF),
        [SMEM] * 2 + [VMEM] * (2 + visits),
        [pltpu.VMEM((visit_count, side, width), BF)],
        flops=20 * visit_count * side * width,
        data=4 * visit_count * side * width,
        name="finish",
    )(basis_choice, coef_table.T, filtered, plane, *own)


def solution(mesh):
    return jax.shard_map(
        on_device,
        mesh=mesh,
        in_specs=(
            P(("group", "visit", "band"), "sky", None, None),
            P(("group", "visit", "band"), "sky", None),
            P(("group", "visit", "band"), "sky"),
            P(),
            P(("group", "visit", "band"), "sky"),
            P("group", "sky", None),
            P(),
            P(("group", "visit", "band"), "sky"),
            P(),
        ),
        out_specs=P(("group", "visit", "band"), "sky", None),
        check_vma=False,
    )
```

```python
import functools
import itertools
import math

import jax
import jax.numpy as jnp
from jax import lax
from jax.experimental import pallas as pl
from jax.experimental.pallas import tpu as pltpu
from jax.sharding import PartitionSpec as P


BF = jnp.bfloat16
F32 = jnp.float32
I32 = jnp.int32
VMEM = pl.BlockSpec(memory_space=pltpu.VMEM)
SMEM = pl.BlockSpec(memory_space=pltpu.SMEM)
HBM = pl.BlockSpec(memory_space=pltpu.HBM)
LABELS = 8


def kernel_call(body, outs, in_specs, scratch=(), flops=0, data=0, out_specs=None):
    def call(*args):
        held = [*args, *jax.tree.leaves(outs), *(s for s in scratch if len(s.shape) > 1)]
        places = out_specs or jax.tree.map(lambda _: VMEM, outs)
        room = sum(math.prod(a.shape) * jnp.dtype(a.dtype).itemsize for a in held)
        return pl.pallas_call(
            body,
            out_shape=outs,
            in_specs=in_specs,
            out_specs=places,
            scratch_shapes=list(scratch),
            cost_estimate=pl.CostEstimate(flops=flops, bytes_accessed=data, transcendentals=0),
            compiler_params=pltpu.CompilerParams(vmem_limit_bytes=room + room // 4 + (4 << 20)),
        )(*args)

    return call


def sinc(x):
    angle = x * jnp.float32(jnp.pi)
    safe = jnp.where(x == 0.0, 1.0, angle)
    return jnp.where(x == 0.0, 1.0, jnp.sin(safe) / safe)


def iota(shape, dim):
    return lax.broadcasted_iota(I32, shape, dim)


def warp_body(patches, visits, cap, *refs):
    sources, parcels, held = refs[:5], refs[5:-9], refs[-9:]
    routes, offsets, entries, table, raw, small, large, seats, labels = held[:9]
    copies = [
        pltpu.make_async_copy(source, target, small.at[n])
        for n, (source, target) in enumerate(zip(sources[:4], held[:4]))
    ]
    groups = large.shape[0]
    per_group = raw.shape[1] // groups
    loads = [
        pltpu.make_async_copy(
            sources[4].at[:, g * per_group : (g + 1) * per_group],
            raw.at[:, g * per_group : (g + 1) * per_group],
            large.at[g],
        )
        for g in range(groups)
    ]
    for copy in copies + loads:
        copy.start()
    visit_count, tile_cols, side, _ = raw.shape
    tiles = visit_count * tile_cols
    part = side // visits
    sky, visit = lax.axis_index("sky"), lax.axis_index("visit")
    for copy in copies:
        copy.wait()
    row = iota((2 * tiles, side), 0)
    shift = jnp.zeros((2 * tiles, side), F32)
    for n in range(tiles):
        v, i = divmod(n, tile_cols)
        entry = entries[v, i]
        for axis in range(2):
            amount = offsets[v, axis, i].astype(F32) + table[axis, entry]
            shift = jnp.where(row == 2 * n + axis, amount, shift)
    lane = iota((2 * tiles, side), 1)
    step = jnp.where(lane < side // 2, lane, lane - side)
    x = jnp.where(row % 2 == 0, -step, step).astype(F32) - shift
    taps = jnp.where(jnp.abs(x) < 3.0, sinc(x) * sinc(x / 3.0), 0.0)
    near = jnp.abs(iota((side, side), 1) - iota((side, side), 0)) < side // 2

    def spread(index):
        rows = jnp.broadcast_to(taps[index : index + 1, :], (side, side))
        rolled = pltpu.roll(rows, 0, 1, stride=1, stride_axis=0)
        return jnp.where(near, rolled, 0.0).astype(BF)

    for k in range(patches):
        labels[k] = jnp.full((LABELS, side), -1.0, F32)
    count = [jnp.int32(0)] * patches
    for i, v in itertools.product(range(tile_cols), range(visit_count)):
        n = v * tile_cols + i
        if v == 0 and i % per_group == 0:
            loads[i // per_group].wait()
        halfway = jnp.dot(spread(2 * n), raw[v, i], preferred_element_type=F32).astype(BF)
        warped = jnp.dot(halfway, spread(2 * n + 1), preferred_element_type=F32).astype(BF)
        route = routes[v, i]
        owner = lax.div(route, tile_cols)
        slot = route - owner * tile_cols
        relative = lax.rem(owner - sky + patches, patches)
        seat = sum(jnp.where(relative == k, count[k], 0) for k in range(patches))
        count = [count[k] + (relative == k).astype(I32) for k in range(patches)]
        seats[relative * cap + seat] = warped
        labels[relative, pl.ds(seat, 1), :] = jnp.full(
            (1, side), ((visit * visit_count + v) * tile_cols + slot).astype(F32), F32
        )
    for k in range(patches):
        for r in range(visits):
            parcel = parcels[k * visits + r]
            target = lax.rem(visit + r, visits)
            rows = pl.ds(pl.multiple_of(target * part, part), part)
            for seat in range(cap):
                parcel[seat * part : (seat + 1) * part, :] = seats[k * cap + seat, rows, :]
            parcel[cap * part :, :] = labels[k].astype(BF)


def warp_tiles(patches, visits, cap, raw, offsets, entries, table, routes):
    visit_count, tile_cols, side, _ = raw.shape
    parcel = jax.ShapeDtypeStruct((cap * (side // visits) + LABELS, side), BF)
    small = [routes, jnp.transpose(offsets, (0, 2, 1)), entries, table.T]
    return kernel_call(
        functools.partial(warp_body, patches, visits, cap),
        [parcel] * (patches * visits),
        [HBM] * 5,
        [pltpu.SMEM(a.shape, a.dtype) for a in small]
        + [
            pltpu.VMEM(raw.shape, BF),
            pltpu.SemaphoreType.DMA((len(small),)),
            pltpu.SemaphoreType.DMA((math.gcd(4, tile_cols),)),
            pltpu.VMEM((patches * cap, side, side), BF),
            pltpu.VMEM((patches, LABELS, side), F32),
        ],
        flops=4 * visit_count * tile_cols * side**3,
        data=4 * raw.size,
    )(*(pltpu.with_memory_space_constraint(a, pltpu.HBM) for a in (*small, raw)))


def tables_body(side, block, choice, coefs, listed, taps, plane, bands, mixes):
    for j, t, b in itertools.product(*map(range, (*choice.shape, coefs.shape[0]))):
        row = (j * choice.shape[1] + t) * coefs.shape[0] + b
        mixes[row : row + 1, :] = jnp.full((1, side), coefs[b, choice[j, t]], F32)
    visit_total, tile_cols, per = listed.shape
    width = visit_total * per
    bad = jnp.concatenate([listed[v] for v in range(visit_total)], axis=1)
    bad_row = lax.div(bad, side)
    bad_col = bad - bad_row * side
    place = iota((side, width), 0)
    weight = (lax.div(iota((side, width), 1), per) + 1).astype(F32)
    for t in range(tile_cols):
        rows = jnp.where(bad_row[t : t + 1, :] == place, 1.0, 0.0).astype(BF)
        cols = jnp.where(bad_col[t : t + 1, :] == place, weight, 0.0).astype(BF)
        plane[:, t * side : (t + 1) * side] = lax.dot_general(
            rows, cols, (((1,), (1,)), ((), ())), preferred_element_type=F32
        )
    bases, pairs, lanes = taps.shape
    for b in range(bases):
        for j in range(pairs):
            rows = jnp.broadcast_to(taps[b, j : j + 1, :], (block, lanes))
            bands[b * block : (b + 1) * block, j * lanes : (j + 1) * lanes] = pltpu.roll(
                rows, 0, 1, stride=1, stride_axis=0
            ).astype(BF)


def make_tables(choice, coefs, listed, kernels, side, block):
    visit_total, tile_cols, per = listed.shape
    bases, taps, _ = kernels.shape
    window = block + taps - 1
    group = max(1, 128 // window)
    padded = -(-taps // group) * group
    columns = jnp.pad(
        jnp.transpose(kernels, (0, 2, 1)).astype(F32), ((0, 0), (0, padded - taps), (0, window - taps))
    ).reshape(bases, padded // group, group * window)
    return kernel_call(
        functools.partial(tables_body, side, block),
        [
            jax.ShapeDtypeStruct((side, tile_cols * side), F32),
            jax.ShapeDtypeStruct((bases * block, padded * window), BF),
            jax.ShapeDtypeStruct((choice.size * bases, side), F32),
        ],
        [SMEM] * 2 + [VMEM] * 2,
        flops=2 * tile_cols * side * side * visit_total * per,
        data=4 * side * side * tile_cols,
    )(choice, coefs.T, listed, columns)


def land_body(visits, bands, visit_count, cap, plane, *refs):
    count = len(refs) - 2 - visits
    parcels, slabs, partial, image = refs[:count], refs[count:-2], refs[-2], refs[-1]
    side = parcels[0].shape[1]
    part = (parcels[0].shape[0] - LABELS) // cap
    tile_cols = image.shape[2] // side
    held = visits * visit_count
    visit, band = lax.axis_index("visit"), lax.axis_index("band")
    for parcel in parcels:
        labels = parcel[cap * part :, :].astype(F32)
        for seat in range(cap):
            label = labels[seat, 0].astype(I32)
            label = jnp.where(label < 0, held * tile_cols, label)
            which = lax.div(label, tile_cols)
            column = (label - which * tile_cols) * side
            image[which, :, pl.ds(pl.multiple_of(column, side), side)] = parcel[
                seat * part : (seat + 1) * part, :
            ]
    mine = plane[pl.ds(pl.multiple_of(visit * part, part), part), :]
    total = jnp.zeros(mine.shape, F32)
    high = jnp.full(mine.shape, -jnp.inf, F32)
    low = jnp.full(mine.shape, jnp.inf, F32)
    for n in range(held):
        own, local = divmod(n, visit_count)
        number = ((own * bands + band) * visit_count + local + 1).astype(F32)
        value = image[n].astype(F32)
        bad = mine == number
        total = total + jnp.where(bad, 0.0, value)
        high = jnp.maximum(high, jnp.where(bad, -jnp.inf, value))
        low = jnp.minimum(low, jnp.where(bad, jnp.inf, value))
    partial[0] = total.astype(BF)
    partial[1] = high.astype(BF)
    partial[2] = low.astype(BF)
    for r in range(visits):
        base = lax.rem(visit + r, visits) * visit_count
        for j in range(visit_count):
            slabs[r][j] = image[base + j]


def land_tiles(visits, bands, visit_count, cap, tile_cols, plane, parcels):
    side = parcels[0].shape[1]
    part = (parcels[0].shape[0] - LABELS) // cap
    width = tile_cols * side
    out = kernel_call(
        functools.partial(land_body, visits, bands, visit_count, cap),
        [jax.ShapeDtypeStruct((visit_count, part, width), BF)] * visits
        + [jax.ShapeDtypeStruct((3, part, width), BF)],
        [VMEM] * (1 + len(parcels)),
        [pltpu.VMEM((visits * visit_count + 1, part, width), BF)],
        flops=10 * visits * visit_count * part * width,
        data=4 * visits * visit_count * part * width,
    )(plane, *parcels)
    return out[:-1], out[-1]


def coadd_body(visit_total, margin, plane, *refs):
    partials, (coadd, edge) = refs[:-2], refs[-2:]
    part = coadd.shape[0]
    visit = lax.axis_index("visit")
    mine = plane[pl.ds(pl.multiple_of(visit * part, part), part), :]
    total, high, low = (partials[0][n].astype(F32) for n in range(3))
    for other in partials[1:]:
        total = total + other[0].astype(F32)
        high = jnp.maximum(high, other[1].astype(F32))
        low = jnp.minimum(low, other[2].astype(F32))
    scale = jnp.where(mine > 0.0, 1.0 / (visit_total - 3.0), 1.0 / (visit_total - 2.0))
    coadd[...] = ((total - high - low) * scale).astype(BF)
    start = pl.multiple_of(jnp.where(visit == 0, 0, part - margin), margin)
    edge[...] = coadd[pl.ds(start, margin), :]


def filter_body(visits, margin, bands, *refs):
    pieces, halos = refs[:visits], refs[visits : visits + 2]
    out, image, moved = refs[visits + 2 :]
    sky, visit, band = (lax.axis_index(name) for name in ("sky", "visit", "band"))
    patches = lax.axis_size("sky")
    part, width = pieces[0].shape
    taps = moved.shape[0]
    mine = lax.rem(visit, 2) == band
    below = jnp.where(mine, halos[0][...], halos[1][...])
    above = jnp.where(mine, halos[1][...], halos[0][...])
    below = jnp.where(sky == patches - 1, jnp.zeros_like(below), below)
    above = jnp.where(sky == 0, jnp.zeros_like(above), above)
    image[:margin, :] = above
    image[margin + visits * part :, :] = below
    for r in range(visits):
        start = pl.multiple_of(lax.rem(visit + r, visits) * part + margin, margin)
        image[pl.ds(start, part), :] = pieces[r][...]
    column = iota((image.shape[0], width), 1)
    zero = jnp.zeros((), BF)
    for dx in range(taps):
        rolled = pltpu.roll(image[...], (margin - dx) % width, 1)
        if dx < margin:
            rolled = jnp.where(column >= margin - dx, rolled, zero)
        elif dx > margin:
            rolled = jnp.where(column < width + margin - dx, rolled, zero)
        moved[dx] = rolled
    blocks = out.shape[0]
    block = visits * part // blocks
    window = block + 2 * margin
    step = min(256, width)
    left = bands[:, : taps * window]
    for n in range(blocks):
        for c in range(0, width, step):
            right = moved[:, n * block : n * block + window, c : c + step].reshape(taps * window, step)
            out[n, :, c : c + step] = jnp.dot(left, right, preferred_element_type=F32).astype(BF)


def finish_body(visits, bands, tile_cols, mixes, filtered, plane, *refs):
    slabs, (out, image, result, sems) = refs[:visits], refs[visits:]
    visit, band = lax.axis_index("visit"), lax.axis_index("band")
    visit_count, part, width = slabs[0].shape
    blocks = filtered.shape[0]
    bases = mixes.shape[0] // (visit_count * tile_cols)
    block = filtered.shape[1] // bases
    side = width // tile_cols
    for r in range(visits):
        start = pl.multiple_of(lax.rem(visit + r, visits) * part, part)
        image[:, pl.ds(start, part), :] = slabs[r][...]
    numbers = [
        ((visit * bands + band) * visit_count + j + 1).astype(F32) for j in range(visit_count)
    ]
    copies = []
    for n in range(blocks):
        rows = slice(n * block, (n + 1) * block)
        for t in range(tile_cols):
            cols = slice(t * side, (t + 1) * side)
            planes = [
                filtered[n, b * block : (b + 1) * block, cols].astype(F32) for b in range(bases)
            ]
            bad = plane[rows, cols]
            for j in range(visit_count):
                row = (j * tile_cols + t) * bases
                template = sum(mixes[row + b : row + b + 1, :] * planes[b] for b in range(bases))
                value = image[j, rows, cols].astype(F32) - template
                result[j, rows, cols] = jnp.where(bad == numbers[j], 0.0, value).astype(BF)
        copies.append(pltpu.make_async_copy(result.at[:, rows], out.at[:, rows], sems.at[n]))
        copies[-1].start()
    for copy in copies:
        copy.wait()


def on_device(
    raw_tiles,
    pixel_offsets,
    shift_entry_index,
    shift_table,
    tile_routes,
    bad_pixels,
    basis_kernels,
    basis_choice,
    coef_table,
):
    visit_count, tile_cols, side = raw_tiles.shape[:3]
    patches, visits, bands = (lax.axis_size(name) for name in ("sky", "visit", "band"))
    cap = (visit_count * tile_cols + patches - 1) // patches + 1
    part, width = side // visits, tile_cols * side
    visit_total = bad_pixels.shape[0]
    bases, taps = basis_kernels.shape[:2]
    margin = taps // 2
    block = 2 * margin

    parcels = warp_tiles(
        patches, visits, cap, raw_tiles, pixel_offsets, shift_entry_index, shift_table, tile_routes
    )
    far = sorted(range(patches), key=lambda k: (-min(k, patches - k), -k))
    order = [k * visits + r for k in far for r in reversed(range(visits)) if k + r > 0]
    arrived = [parcels[0]]
    for n in order:
        k, r = divmod(n, visits)
        pairs = [
            (s * visits + v, (s + k) % patches * visits + (v + r) % visits)
            for s in range(patches)
            for v in range(visits)
        ]
        arrived.append(lax.ppermute(parcels[n], ("sky", "visit"), pairs))
    plane, toeplitz, mixes = make_tables(
        basis_choice, coef_table, bad_pixels, basis_kernels, side, block
    )
    slabs, partial = land_tiles(visits, bands, visit_count, cap, tile_cols, plane, arrived)

    partials = [partial] + [
        lax.ppermute(partial, "band", [(b, (b + q) % bands) for b in range(bands)])
        for q in range(1, bands)
    ]
    coadd, edge = kernel_call(
        functools.partial(coadd_body, visit_total, margin),
        [jax.ShapeDtypeStruct((part, width), BF), jax.ShapeDtypeStruct((margin, width), BF)],
        [VMEM] * (1 + bands),
        flops=8 * part * width,
        data=8 * part * width,
    )(plane, *partials)

    def turn(r):
        return [(v, (v - r) % visits) for v in range(visits)]

    pieces = [coadd] + [lax.ppermute(coadd, "visit", turn(r)) for r in range(1, visits)]
    halos = []
    for first in range(0, visits, bands):
        pairs = []
        for s, b in itertools.product(range(patches), range(bands)):
            r = first + b
            top = ((s - 1) % patches, r)
            bottom = ((s + 1) % patches, visits - 1 - r)
            for v, (to_s, to_v) in ((0, top), (visits - 1, bottom)):
                pairs.append(((s * visits + v) * bands + b, (to_s * visits + to_v) * bands + b))
        halos.append(lax.ppermute(edge, ("sky", "visit", "band"), pairs))
    halo = functools.reduce(jnp.add, halos)
    halos = [halo, lax.ppermute(halo, "band", [(b, (b + 1) % bands) for b in range(bands)])]
    own = [slabs[0]] + [
        lax.ppermute(slabs[r], "visit", [(v, (v + r) % visits) for v in range(visits)])
        for r in range(1, visits)
    ]
    own = [own[0]] + [own[visits - r] for r in range(1, visits)]
    filtered = kernel_call(
        functools.partial(filter_body, visits, margin),
        jax.ShapeDtypeStruct((side // block, bases * block, width), BF),
        [VMEM] * (3 + visits),
        [
            pltpu.VMEM((side + 2 * margin, width), BF),
            pltpu.VMEM((taps, side + 2 * margin, width), BF),
        ],
        flops=2 * bases * side * width * taps * (block + taps - 1),
        data=2 * bases * side * width,
    )(toeplitz, *pieces, *halos)
    return kernel_call(
        functools.partial(finish_body, visits, bands, tile_cols),
        jax.ShapeDtypeStruct((visit_count, side, width), BF),
        [VMEM] * (3 + visits),
        [
            pltpu.VMEM((visit_count, side, width), BF),
            pltpu.VMEM((visit_count, side, width), BF),
            pltpu.SemaphoreType.DMA((side // block,)),
        ],
        flops=20 * visit_count * side * width,
        data=4 * visit_count * side * width,
        out_specs=HBM,
    )(mixes, filtered, plane, *own)


def solution(mesh):
    return jax.shard_map(
        on_device,
        mesh=mesh,
        in_specs=(
            P(("group", "visit", "band"), "sky", None, None),
            P(("group", "visit", "band"), "sky", None),
            P(("group", "visit", "band"), "sky"),
            P(),
            P(("group", "visit", "band"), "sky"),
            P("group", "sky", None),
            P(),
            P(("group", "visit", "band"), "sky"),
            P(),
        ),
        out_specs=P(("group", "visit", "band"), "sky", None),
        check_vma=False,
    )
```

```python
import functools
import itertools
import math

import jax
import jax.numpy as jnp
from jax import lax
from jax.experimental import pallas as pl
from jax.experimental.pallas import tpu as pltpu
from jax.sharding import PartitionSpec as P


BF = jnp.bfloat16
F32 = jnp.float32
I32 = jnp.int32
VMEM = pl.BlockSpec(memory_space=pltpu.VMEM)
SMEM = pl.BlockSpec(memory_space=pltpu.SMEM)
HBM = pl.BlockSpec(memory_space=pltpu.HBM)
LABELS = 8


def kernel_call(body, outs, in_specs, scratch=(), flops=0, data=0, out_specs=None, spare=4):
    def call(*args):
        held = [*args, *jax.tree.leaves(outs), *(s for s in scratch if len(s.shape) > 1)]
        places = out_specs or jax.tree.map(lambda _: VMEM, outs)
        room = sum(math.prod(a.shape) * jnp.dtype(a.dtype).itemsize for a in held)
        return pl.pallas_call(
            body,
            out_shape=outs,
            in_specs=in_specs,
            out_specs=places,
            scratch_shapes=list(scratch),
            cost_estimate=pl.CostEstimate(flops=flops, bytes_accessed=data, transcendentals=0),
            compiler_params=pltpu.CompilerParams(vmem_limit_bytes=room + room // 4 + (spare << 20)),
        )(*args)

    return call


def sinc(x):
    angle = x * jnp.float32(jnp.pi)
    safe = jnp.where(x == 0.0, 1.0, angle)
    return jnp.where(x == 0.0, 1.0, jnp.sin(safe) / safe)


def iota(shape, dim):
    return lax.broadcasted_iota(I32, shape, dim)


def warp_body(patches, visits, cap, *refs):
    sources, parcels, held = refs[:5], refs[5:-10], refs[-10:]
    routes, offsets, entries, table, raw, small, large, seats, labels, weights = held
    copies = [
        pltpu.make_async_copy(source, target, small.at[n])
        for n, (source, target) in enumerate(zip(sources[:4], held[:4]))
    ]
    groups = large.shape[0]
    per_group = raw.shape[1] // groups
    loads = [
        pltpu.make_async_copy(
            sources[4].at[:, g * per_group : (g + 1) * per_group],
            raw.at[:, g * per_group : (g + 1) * per_group],
            large.at[g],
        )
        for g in range(groups)
    ]
    for copy in copies + loads:
        copy.start()
    visit_count, tile_cols, side, _ = raw.shape
    tiles = visit_count * tile_cols
    part = side // visits
    sky, visit = lax.axis_index("sky"), lax.axis_index("visit")
    for copy in copies:
        copy.wait()
    row = iota((2 * tiles, side), 0)
    shift = jnp.zeros((2 * tiles, side), F32)
    for n in range(tiles):
        v, i = divmod(n, tile_cols)
        entry = entries[v, i]
        for axis in range(2):
            amount = offsets[v, axis, i].astype(F32) + table[axis, entry]
            shift = jnp.where(row == 2 * n + axis, amount, shift)
    lane = iota((2 * tiles, side), 1)
    step = jnp.where(lane < side // 2, lane, lane - side)
    x = jnp.where(row % 2 == 0, -step, step).astype(F32) - shift
    taps = jnp.where(jnp.abs(x) < 3.0, sinc(x) * sinc(x / 3.0), 0.0)
    near = jnp.abs(iota((side, side), 1) - iota((side, side), 0)) < side // 2

    def spread(index):
        rows = jnp.broadcast_to(taps[index : index + 1, :], (side, side))
        rolled = pltpu.roll(rows, 0, 1, stride=1, stride_axis=0)
        return jnp.where(near, rolled, 0.0).astype(BF)

    for n in range(2 * tiles):
        weights[n] = spread(n)
    for k in range(patches):
        labels[k] = jnp.full((LABELS, side), -1.0, F32)
    count = [jnp.int32(0)] * patches
    for load in loads:
        load.wait()
    for i, v in itertools.product(range(tile_cols), range(visit_count)):
        n = v * tile_cols + i
        halfway = jnp.dot(weights[2 * n], raw[v, i], preferred_element_type=F32).astype(BF)
        warped = jnp.dot(halfway, weights[2 * n + 1], preferred_element_type=F32).astype(BF)
        route = routes[v, i]
        owner = lax.div(route, tile_cols)
        slot = route - owner * tile_cols
        relative = lax.rem(owner - sky + patches, patches)
        seat = sum(jnp.where(relative == k, count[k], 0) for k in range(patches))
        count = [count[k] + (relative == k).astype(I32) for k in range(patches)]
        seats[relative * cap + seat] = warped
        labels[relative, pl.ds(seat, 1), :] = jnp.full(
            (1, side), ((visit * visit_count + v) * tile_cols + slot).astype(F32), F32
        )
    for k in range(patches):
        for r in range(visits):
            parcel = parcels[k * visits + r]
            target = lax.rem(visit + r, visits)
            rows = pl.ds(pl.multiple_of(target * part, part), part)
            for seat in range(cap):
                parcel[seat * part : (seat + 1) * part, :] = seats[k * cap + seat, rows, :]
            parcel[cap * part :, :] = labels[k].astype(BF)


def warp_tiles(patches, visits, cap, raw, offsets, entries, table, routes):
    visit_count, tile_cols, side, _ = raw.shape
    parcel = jax.ShapeDtypeStruct((cap * (side // visits) + LABELS, side), BF)
    small = [routes, jnp.transpose(offsets, (0, 2, 1)), entries, table.T]
    return kernel_call(
        functools.partial(warp_body, patches, visits, cap),
        [parcel] * (patches * visits),
        [HBM] * 5,
        [pltpu.SMEM(a.shape, a.dtype) for a in small]
        + [
            pltpu.VMEM(raw.shape, BF),
            pltpu.SemaphoreType.DMA((len(small),)),
            pltpu.SemaphoreType.DMA((math.gcd(4, tile_cols),)),
            pltpu.VMEM((patches * cap, side, side), BF),
            pltpu.VMEM((patches, LABELS, side), F32),
            pltpu.VMEM((2 * visit_count * tile_cols, side, side), BF),
        ],
        flops=4 * visit_count * tile_cols * side**3,
        data=4 * raw.size,
    )(*(pltpu.with_memory_space_constraint(a, pltpu.HBM) for a in (*small, raw)))


def tables_body(side, block, choice, coefs, listed, taps, heads, tails, plane, bands, mixes, ends):
    for j, t, b in itertools.product(*map(range, (*choice.shape, coefs.shape[0]))):
        row = (j * choice.shape[1] + t) * coefs.shape[0] + b
        mixes[row : row + 1, :] = jnp.full((1, side), coefs[b, choice[j, t]], F32)
    visit_total, tile_cols, per = listed.shape
    width = visit_total * per
    bad = jnp.concatenate([listed[v] for v in range(visit_total)], axis=1)
    bad_row = lax.div(bad, side)
    bad_col = bad - bad_row * side
    place = iota((side, width), 0)
    weight = (lax.div(iota((side, width), 1), per) + 1).astype(F32)
    for t in range(tile_cols):
        rows = jnp.where(bad_row[t : t + 1, :] == place, 1.0, 0.0).astype(BF)
        cols = jnp.where(bad_col[t : t + 1, :] == place, weight, 0.0).astype(BF)
        plane[:, t * side : (t + 1) * side] = lax.dot_general(
            rows, cols, (((1,), (1,)), ((), ())), preferred_element_type=F32
        )
    bases, pairs, lanes = taps.shape
    for b in range(bases):
        for j in range(pairs):
            rows = jnp.broadcast_to(taps[b, j : j + 1, :], (block, lanes))
            bands[b * block : (b + 1) * block, j * lanes : (j + 1) * lanes] = pltpu.roll(
                rows, 0, 1, stride=1, stride_axis=0
            ).astype(BF)
    margin = block // 2
    row, place = iota((block, lanes), 0), lax.rem(iota((block, lanes), 1), margin)
    for n, (source, shift, fits) in enumerate(
        ((heads, 0, place >= row), (tails, lanes - 2 * margin + 1, place <= row - margin))
    ):
        for b, j in itertools.product(range(bases), range(source.shape[1])):
            rows = jnp.broadcast_to(source[b, j : j + 1, :], (block, lanes))
            rolled = pltpu.roll(rows, shift, 1, stride=1, stride_axis=0)
            ends[n, b * block : (b + 1) * block, j * lanes : (j + 1) * lanes] = jnp.where(
                fits, rolled, 0.0
            ).astype(BF)


def make_tables(choice, coefs, listed, kernels, side, block):
    visit_total, tile_cols, per = listed.shape
    bases, taps, _ = kernels.shape
    window = block + taps - 1
    group = max(1, 128 // window)
    padded = -(-taps // group) * group
    turned = jnp.transpose(kernels, (0, 2, 1)).astype(F32)
    columns = jnp.pad(turned, ((0, 0), (0, padded - taps), (0, window - taps))).reshape(
        bases, padded // group, group * window
    )
    margin, lanes = taps // 2, group * window
    groups = -(-taps * margin // lanes)
    fill = ((0, 0), (0, groups * lanes // margin - taps), (0, 0))
    heads, tails = (
        jnp.pad(part, fill).reshape(bases, groups, lanes)
        for part in (turned[:, :, :margin], turned[:, :, margin + 1 :])
    )
    return kernel_call(
        functools.partial(tables_body, side, block),
        [
            jax.ShapeDtypeStruct((side, tile_cols * side), F32),
            jax.ShapeDtypeStruct((bases * block, padded * window), BF),
            jax.ShapeDtypeStruct((choice.size * bases, side), F32),
            jax.ShapeDtypeStruct((2, bases * block, groups * lanes), BF),
        ],
        [SMEM] * 2 + [VMEM] * 4,
        flops=2 * tile_cols * side * side * visit_total * per,
        data=4 * side * side * tile_cols,
    )(choice, coefs.T, listed, columns, heads, tails)


def place(parcels, cap, part, image, of):
    side = parcels[0].shape[1]
    tile_cols, dummy = image.shape[2] // side, image.shape[0] - 1
    for parcel in parcels:
        labels = parcel[cap * part :, :].astype(F32)
        for seat in range(cap):
            label = labels[seat, 0].astype(I32)
            number = lax.div(jnp.maximum(label, 0), tile_cols)
            column = jnp.where(label < 0, 0, label - number * tile_cols) * side
            which = jnp.where(label < 0, dummy, of(number))
            image[which, :, pl.ds(pl.multiple_of(column, side), side)] = parcel[
                seat * part : (seat + 1) * part, :
            ]


def land_body(visits, bands, visit_count, cap, plane, *refs):
    parcels, (slab, partial, image) = refs[:-3], refs[-3:]
    part = slab.shape[1]
    held = visits * visit_count
    visit, band = lax.axis_index("visit"), lax.axis_index("band")
    place(parcels, cap, part, image, lambda number: number)
    mine = plane[pl.ds(pl.multiple_of(visit * part, part), part), :]
    total = jnp.zeros(mine.shape, F32)
    high = jnp.full(mine.shape, -jnp.inf, F32)
    low = jnp.full(mine.shape, jnp.inf, F32)
    for n in range(held):
        own, local = divmod(n, visit_count)
        number = ((own * bands + band) * visit_count + local + 1).astype(F32)
        value = image[n].astype(F32)
        bad = mine == number
        total = total + jnp.where(bad, 0.0, value)
        high = jnp.maximum(high, jnp.where(bad, -jnp.inf, value))
        low = jnp.minimum(low, jnp.where(bad, jnp.inf, value))
    partial[0] = total.astype(BF)
    partial[1] = high.astype(BF)
    partial[2] = low.astype(BF)
    for j in range(visit_count):
        slab[j] = image[visit * visit_count + j]


def land_tiles(visits, bands, visit_count, cap, tile_cols, plane, parcels):
    side = parcels[0].shape[1]
    part = (parcels[0].shape[0] - LABELS) // cap
    width = tile_cols * side
    return kernel_call(
        functools.partial(land_body, visits, bands, visit_count, cap),
        [
            jax.ShapeDtypeStruct((visit_count, part, width), BF),
            jax.ShapeDtypeStruct((3, part, width), BF),
        ],
        [VMEM] * (1 + len(parcels)),
        [pltpu.VMEM((visits * visit_count + 1, part, width), BF)],
        flops=10 * visits * visit_count * part * width,
        data=4 * visits * visit_count * part * width,
    )(plane, *parcels)


def coadd_body(visit_total, margin, plane, *refs):
    partials, (coadd, share, edge) = refs[:-3], refs[-3:]
    part, some = coadd.shape[0], share.shape[0]
    visit, band = lax.axis_index("visit"), lax.axis_index("band")
    mine = plane[pl.ds(pl.multiple_of(visit * part, part), part), :]
    total, high, low = (partials[0][n].astype(F32) for n in range(3))
    for other in partials[1:]:
        total = total + other[0].astype(F32)
        high = jnp.maximum(high, other[1].astype(F32))
        low = jnp.minimum(low, other[2].astype(F32))
    scale = jnp.where(mine > 0.0, 1.0 / (visit_total - 3.0), 1.0 / (visit_total - 2.0))
    coadd[...] = ((total - high - low) * scale).astype(BF)
    share[...] = coadd[pl.ds(pl.multiple_of(band * some, some), some), :]
    start = pl.multiple_of(jnp.where(visit == 0, 0, part - margin), margin)
    edge[...] = coadd[pl.ds(start, margin), :]


def shifted(image, margin, taps, side, first, until):
    rows, width = image.shape
    lane = iota((rows, side), 1)
    blank = jnp.zeros((rows, side), BF)
    shifts = []
    for dx in range(taps):
        shift = dx - margin
        low, high = (first - 1, until) if shift < 0 else (first, until + 1)
        turned = {
            t: pltpu.roll(image[:, t * side : (t + 1) * side], -shift % side, 1)
            if 0 <= t < width // side
            else blank
            for t in range(low, high)
        } if shift else {}
        tiles = []
        for t in range(first, until):
            if shift < 0:
                tiles.append(jnp.where(lane < -shift, turned[t - 1], turned[t]))
            elif shift > 0:
                tiles.append(jnp.where(lane < side - shift, turned[t], turned[t + 1]))
            else:
                tiles.append(image[:, t * side : (t + 1) * side])
        shifts.append(jnp.concatenate(tiles, axis=1))
    return shifts


def apply_rows(left, shifts, pick):
    right = jnp.concatenate([pick(each) for each in shifts], axis=0)
    return jnp.dot(left, right, preferred_element_type=F32)


def collect_body(visits, visit_count, cap, *refs):
    count = len(refs) - (visits - 1)
    parcels, others = refs[:count], refs[count:]
    each = count // (visits - 1)
    part = others[0].shape[1]
    for r, other in enumerate(others):
        place(
            parcels[r * each : (r + 1) * each],
            cap,
            part,
            other,
            lambda number: lax.rem(number, visit_count),
        )


def filter_ahead_body(margin, taps, side, per, bands, own, sums, image):
    part, width = own.shape
    block = 2 * margin
    window = block + taps - 1
    image[:margin] = jnp.zeros((margin, width), BF)
    image[margin + part :] = jnp.zeros((margin, width), BF)
    image[margin : margin + part] = own[...]
    left = bands[:, : taps * window]
    for t in range(0, width // side, per):
        shifts = shifted(image, margin, taps, side, t, t + per)
        for n in range(part // block):
            rows = slice(n * block, n * block + window)
            sums[n, :, t * side : (t + per) * side] = apply_rows(left, shifts, lambda x: x[rows])


def joined(pieces, halos, place_piece):
    sky, visit, band = (lax.axis_index(name) for name in ("sky", "visit", "band"))
    patches, visits = lax.axis_size("sky"), lax.axis_size("visit")
    for n, piece in enumerate(pieces):
        some = piece.shape[0]
        place_piece(lax.rem(visit + 1 + n // 2, visits), lax.rem(band + n, 2) * some, piece[...])
    mine = lax.rem(visit, 2) == band
    below = jnp.where(mine, halos[0][...], halos[1][...])
    above = jnp.where(mine, halos[1][...], halos[0][...])
    below = jnp.where(sky == patches - 1, jnp.zeros_like(below), below)
    above = jnp.where(sky == 0, jnp.zeros_like(above), above)
    return above, below


def render_body(
    margin, taps, tile_cols, per, bands, ends, mixes, plane, sums, own, slab, others, *refs
):
    part, width = own.shape
    pieces, halos, (out, result, sems, image) = refs[:-6], refs[-6:-4], refs[-4:]
    block, step = 2 * margin, per * (width // tile_cols)
    window, blocks = block + taps - 1, part // block
    visit_count, side = result.shape[0], width // tile_cols
    bases = bands.shape[0] // block
    visit, band = lax.axis_index("visit"), lax.axis_index("band")
    band_count = lax.axis_size("band")
    first = visit == 0

    def put(_, start, piece):
        rows = pl.ds(pl.multiple_of(start + margin, margin), piece.shape[0])
        image[rows, :] = piece

    above, below = joined(pieces, halos, put)
    image[:margin] = jnp.where(first, own[part - margin :, :], above)
    image[margin + part : 2 * margin + part] = jnp.where(first, below, own[:margin, :])
    image[2 * margin + part :] = jnp.where(first, above, below)
    edge = slice(part + 2 * margin, part + 3 * margin)

    def before(x):
        return jnp.where(first, x[edge], x[part : part + margin])

    def after(x):
        return jnp.where(first, x[margin : 2 * margin], x[edge])

    numbers = [
        ((visit * band_count + band) * visit_count + j + 1).astype(F32)
        for j in range(visit_count)
    ]
    left = bands[:, : taps * window]

    def finish(start, n, c, source, value):
        value = value.astype(BF).astype(F32)
        rows = pl.ds(pl.multiple_of(start + n * block, block), block)
        for t in range(c * step // side, (c + 1) * step // side):
            cols = slice(t * side, (t + 1) * side)
            inset = slice(t * side - c * step, (t + 1) * side - c * step)
            planes = [value[b * block : (b + 1) * block, inset] for b in range(bases)]
            bad = plane[rows, cols]
            for j in range(visit_count):
                row = (j * tile_cols + t) * bases
                template = sum(mixes[row + b : row + b + 1, :] * planes[b] for b in range(bases))
                pixels = source[j, n * block : (n + 1) * block, cols].astype(F32) - template
                result[j, rows, cols] = jnp.where(bad == numbers[j], 0.0, pixels).astype(BF)

    copies = []
    for c in range(width // step):
        cols = slice(c * step, (c + 1) * step)
        shifts = shifted(image, margin, taps, side, c * per, (c + 1) * per)
        for n in range(blocks):
            rows = slice(n * block, n * block + window)
            value = apply_rows(left, shifts, lambda x: x[rows])
            finish((1 - visit) * part, n, c, others, value)
        for n in range(blocks):
            value = sums[n, :, cols]
            if n == 0:
                value += apply_rows(ends[0, :, : taps * margin], shifts, before)
            if n == blocks - 1:
                value += apply_rows(ends[1, :, : taps * margin], shifts, after)
            finish(visit * part, n, c, slab, value)
        copies.append(
            pltpu.make_async_copy(result.at[:, :, cols], out.at[:, :, cols], sems.at[c])
        )
        copies[-1].start()
    for copy in copies:
        copy.wait()


def filter_body(margin, taps, side, per, bands, own, *refs):
    pieces, halos, (out, image) = refs[:-4], refs[-4:-2], refs[-2:]
    part, width = own.shape
    block = 2 * margin
    window = block + taps - 1

    def put(turn, start, piece):
        start = pl.multiple_of(turn * part + start + margin, margin)
        image[pl.ds(start, piece.shape[0])] = piece

    above, below = joined(pieces, halos, put)
    image[:margin] = above
    image[image.shape[0] - margin :] = below
    put(lax.axis_index("visit"), 0, own[...])
    for t in range(0, width // side, per):
        shifts = shifted(image, margin, taps, side, t, t + per)
        for n in range(out.shape[0]):
            rows = slice(n * block, n * block + window)
            value = apply_rows(bands[:, : taps * window], shifts, lambda x: x[rows])
            out[n, :, t * side : (t + per) * side] = value.astype(BF)


def finish_body(visits, bands, tile_cols, mixes, filtered, plane, *refs):
    slabs, (out, image, result, sems) = refs[:-4], refs[-4:]
    visit, band = lax.axis_index("visit"), lax.axis_index("band")
    part, width = slabs[0].shape[1:]
    visit_count = image.shape[0]
    blocks = filtered.shape[0]
    bases = mixes.shape[0] // (visit_count * tile_cols)
    block = filtered.shape[1] // bases
    side = width // tile_cols
    for r in range(visits):
        start = pl.multiple_of(lax.rem(visit + r, visits) * part, part)
        for j in range(visit_count):
            image[j, pl.ds(start, part), :] = slabs[r][j]
    numbers = [
        ((visit * bands + band) * visit_count + j + 1).astype(F32) for j in range(visit_count)
    ]
    copies = []
    for n in range(blocks):
        rows = slice(n * block, (n + 1) * block)
        for t in range(tile_cols):
            cols = slice(t * side, (t + 1) * side)
            planes = [
                filtered[n, b * block : (b + 1) * block, cols].astype(F32) for b in range(bases)
            ]
            bad = plane[rows, cols]
            for j in range(visit_count):
                row = (j * tile_cols + t) * bases
                template = sum(mixes[row + b : row + b + 1, :] * planes[b] for b in range(bases))
                value = image[j, rows, cols].astype(F32) - template
                result[j, rows, cols] = jnp.where(bad == numbers[j], 0.0, value).astype(BF)
        copies.append(pltpu.make_async_copy(result.at[:, rows], out.at[:, rows], sems.at[n]))
        copies[-1].start()
    for copy in copies:
        copy.wait()


def on_device(
    raw_tiles,
    pixel_offsets,
    shift_entry_index,
    shift_table,
    tile_routes,
    bad_pixels,
    basis_kernels,
    basis_choice,
    coef_table,
):
    visit_count, tile_cols, side = raw_tiles.shape[:3]
    patches, visits, bands = (lax.axis_size(name) for name in ("sky", "visit", "band"))
    cap = (visit_count * tile_cols + patches - 1) // patches + 1
    part, width = side // visits, tile_cols * side
    visit_total = bad_pixels.shape[0]
    bases, taps = basis_kernels.shape[:2]
    margin = taps // 2
    block = 2 * margin

    parcels = warp_tiles(
        patches, visits, cap, raw_tiles, pixel_offsets, shift_entry_index, shift_table, tile_routes
    )
    far = sorted(range(patches), key=lambda k: (-min(k, patches - k), -k))
    order = [k * visits + r for r in reversed(range(visits)) for k in far if k + r > 0]
    arrived = {0: parcels[0]}
    for n in order:
        k, r = divmod(n, visits)
        pairs = [
            (s * visits + v, (s + k) % patches * visits + (v + r) % visits)
            for s in range(patches)
            for v in range(visits)
        ]
        arrived[n] = lax.ppermute(parcels[n], ("sky", "visit"), pairs)
    own_others = []
    for r in range(1, visits):
        own_others.append(parcels[r])
        for k in (k for k in far if k > 0):
            own_others.append(
                lax.ppermute(
                    arrived[k * visits + r], "visit", [(v, (v - r) % visits) for v in range(visits)]
                )
            )
    plane, toeplitz, mixes, ends = make_tables(
        basis_choice, coef_table, bad_pixels, basis_kernels, side, block
    )
    slab, partial = land_tiles(
        visits, bands, visit_count, cap, tile_cols, plane, list(arrived.values())
    )

    partials = [partial] + [
        lax.ppermute(partial, "band", [(b, (b + q) % bands) for b in range(bands)])
        for q in range(1, bands)
    ]
    coadd, share, edge = kernel_call(
        functools.partial(coadd_body, visit_total, margin),
        [jax.ShapeDtypeStruct((rows, width), BF) for rows in (part, part // bands, margin)],
        [VMEM] * (1 + bands),
        flops=8 * part * width,
        data=8 * part * width,
    )(plane, *partials)

    def turn(r):
        return [(v, (v - r) % visits) for v in range(visits)]

    swap = [(b, (b + 1) % bands) for b in range(bands)]
    pieces = []
    for r in range(1, visits):
        pieces.append(lax.ppermute(share, "visit", turn(r)))
        pieces.append(lax.ppermute(pieces[-1], "band", swap))
    halos = []
    for first in range(0, visits, bands):
        pairs = []
        for s, b in itertools.product(range(patches), range(bands)):
            r = first + b
            top = ((s - 1) % patches, r)
            bottom = ((s + 1) % patches, visits - 1 - r)
            for v, (to_s, to_v) in ((0, top), (visits - 1, bottom)):
                pairs.append(((s * visits + v) * bands + b, (to_s * visits + to_v) * bands + b))
        halos.append(lax.ppermute(edge, ("sky", "visit", "band"), pairs))
    halo = functools.reduce(jnp.add, halos)
    halos = [halo, lax.ppermute(halo, "band", swap)]
    others = kernel_call(
        functools.partial(collect_body, visits, visit_count, cap),
        [jax.ShapeDtypeStruct((visit_count + 1, part, width), BF)] * (visits - 1),
        [VMEM] * len(own_others),
        flops=part * width,
        data=4 * visit_count * side * width,
    )(*own_others)
    work = 2 * bases * side * width * taps * (block + taps - 1)
    per = tile_cols
    result = jax.ShapeDtypeStruct((visit_count, side, width), BF)
    if visits == 2 and part % block == 0:
        sums = kernel_call(
            functools.partial(filter_ahead_body, margin, taps, side, per),
            jax.ShapeDtypeStruct((part // block, bases * block, width), F32),
            [VMEM] * 2,
            [pltpu.VMEM((part + 2 * margin, width), BF)],
            flops=work // 2,
            data=4 * bases * part * width,
            spare=24,
        )(toeplitz, coadd)
        return kernel_call(
            functools.partial(render_body, margin, taps, tile_cols, per),
            result,
            [VMEM] * (8 + len(pieces) + 2),
            [
                pltpu.VMEM(result.shape, BF),
                pltpu.SemaphoreType.DMA((tile_cols // per,)),
                pltpu.VMEM((part + 3 * margin, width), BF),
            ],
            flops=work // 2,
            data=2 * bases * side * width,
            spare=24,
            out_specs=HBM,
        )(toeplitz, ends, mixes, plane, sums, coadd, slab, *others, *pieces, *halos)
    filtered = kernel_call(
        functools.partial(filter_body, margin, taps, side, per),
        jax.ShapeDtypeStruct((side // block, bases * block, width), BF),
        [VMEM] * (2 + len(pieces) + 2),
        [pltpu.VMEM((side + 2 * margin, width), BF)],
        flops=work,
        data=2 * bases * side * width,
        spare=24,
    )(toeplitz, coadd, *pieces, *halos)
    return kernel_call(
        functools.partial(finish_body, visits, bands, tile_cols),
        result,
        [VMEM] * (3 + visits),
        [
            pltpu.VMEM(result.shape, BF),
            pltpu.VMEM(result.shape, BF),
            pltpu.SemaphoreType.DMA((side // block,)),
        ],
        flops=20 * visit_count * side * width,
        data=4 * visit_count * side * width,
        out_specs=HBM,
    )(mixes, filtered, plane, slab, *others)


def solution(mesh):
    return jax.shard_map(
        on_device,
        mesh=mesh,
        in_specs=(
            P(("group", "visit", "band"), "sky", None, None),
            P(("group", "visit", "band"), "sky", None),
            P(("group", "visit", "band"), "sky"),
            P(),
            P(("group", "visit", "band"), "sky"),
            P("group", "sky", None),
            P(),
            P(("group", "visit", "band"), "sky"),
            P(),
        ),
        out_specs=P(("group", "visit", "band"), "sky", None),
        check_vma=False,
    )
```

```python
import functools
import itertools
import math

import jax
import jax.numpy as jnp
from jax import lax
from jax.experimental import pallas as pl
from jax.experimental.pallas import tpu as pltpu
from jax.sharding import PartitionSpec as P


BF = jnp.bfloat16
F32 = jnp.float32
I32 = jnp.int32
VMEM = pl.BlockSpec(memory_space=pltpu.VMEM)
SMEM = pl.BlockSpec(memory_space=pltpu.SMEM)
HBM = pl.BlockSpec(memory_space=pltpu.HBM)
LABELS = 8


def kernel_call(body, outs, in_specs, scratch=(), flops=0, data=0, out_specs=None, spare=4):
    def call(*args):
        held = [*args, *jax.tree.leaves(outs), *(s for s in scratch if len(s.shape) > 1)]
        places = out_specs or jax.tree.map(lambda _: VMEM, outs)
        room = sum(math.prod(a.shape) * jnp.dtype(a.dtype).itemsize for a in held)
        return pl.pallas_call(
            body,
            out_shape=outs,
            in_specs=in_specs,
            out_specs=places,
            scratch_shapes=list(scratch),
            cost_estimate=pl.CostEstimate(flops=flops, bytes_accessed=data, transcendentals=0),
            compiler_params=pltpu.CompilerParams(vmem_limit_bytes=room + room // 4 + (spare << 20)),
        )(*args)

    return call


def sinc(x):
    angle = x * jnp.float32(jnp.pi)
    safe = jnp.where(x == 0.0, 1.0, angle)
    return jnp.where(x == 0.0, 1.0, jnp.sin(safe) / safe)


def iota(shape, dim):
    return lax.broadcasted_iota(I32, shape, dim)


def warp_body(patches, visits, cap, *refs):
    sources, parcels, held = refs[:5], refs[5:-10], refs[-10:]
    routes, offsets, entries, table, raw, small, large, seats, labels, weights = held
    copies = [
        pltpu.make_async_copy(source, target, small.at[n])
        for n, (source, target) in enumerate(zip(sources[:4], held[:4]))
    ]
    groups = large.shape[0]
    per_group = raw.shape[1] // groups
    loads = [
        pltpu.make_async_copy(
            sources[4].at[:, g * per_group : (g + 1) * per_group],
            raw.at[:, g * per_group : (g + 1) * per_group],
            large.at[g],
        )
        for g in range(groups)
    ]
    for copy in copies + loads:
        copy.start()
    visit_count, tile_cols, side, _ = raw.shape
    tiles = visit_count * tile_cols
    part = side // visits
    sky, visit = lax.axis_index("sky"), lax.axis_index("visit")
    for copy in copies:
        copy.wait()
    row = iota((2 * tiles, side), 0)
    shift = jnp.zeros((2 * tiles, side), F32)
    for n in range(tiles):
        v, i = divmod(n, tile_cols)
        entry = entries[v, i]
        for axis in range(2):
            amount = offsets[v, axis, i].astype(F32) + table[axis, entry]
            shift = jnp.where(row == 2 * n + axis, amount, shift)
    lane = iota((2 * tiles, side), 1)
    step = jnp.where(lane < side // 2, lane, lane - side)
    x = jnp.where(row % 2 == 0, -step, step).astype(F32) - shift
    taps = jnp.where(jnp.abs(x) < 3.0, sinc(x) * sinc(x / 3.0), 0.0)
    near = jnp.abs(iota((side, side), 1) - iota((side, side), 0)) < side // 2

    def spread(index):
        rows = jnp.broadcast_to(taps[index : index + 1, :], (side, side))
        rolled = pltpu.roll(rows, 0, 1, stride=1, stride_axis=0)
        return jnp.where(near, rolled, 0.0).astype(BF)

    for n in range(2 * tiles):
        weights[n] = spread(n)
    for k in range(patches):
        labels[k] = jnp.full((LABELS, side), -1.0, F32)
    count = [jnp.int32(0)] * patches
    for load in loads:
        load.wait()
    for i, v in itertools.product(range(tile_cols), range(visit_count)):
        n = v * tile_cols + i
        halfway = jnp.dot(weights[2 * n], raw[v, i], preferred_element_type=F32).astype(BF)
        warped = jnp.dot(halfway, weights[2 * n + 1], preferred_element_type=F32).astype(BF)
        route = routes[v, i]
        owner = lax.div(route, tile_cols)
        slot = route - owner * tile_cols
        relative = lax.rem(owner - sky + patches, patches)
        seat = sum(jnp.where(relative == k, count[k], 0) for k in range(patches))
        count = [count[k] + (relative == k).astype(I32) for k in range(patches)]
        seats[relative * cap + seat] = warped
        labels[relative, pl.ds(seat, 1), :] = jnp.full(
            (1, side), ((visit * visit_count + v) * tile_cols + slot).astype(F32), F32
        )
    for k in range(patches):
        for r in range(visits):
            parcel = parcels[k * visits + r]
            target = lax.rem(visit + r, visits)
            rows = pl.ds(pl.multiple_of(target * part, part), part)
            for seat in range(cap):
                parcel[seat * part : (seat + 1) * part, :] = seats[k * cap + seat, rows, :]
            parcel[cap * part :, :] = labels[k].astype(BF)


def warp_tiles(patches, visits, cap, raw, offsets, entries, table, routes):
    visit_count, tile_cols, side, _ = raw.shape
    parcel = jax.ShapeDtypeStruct((cap * (side // visits) + LABELS, side), BF)
    small = [routes, jnp.transpose(offsets, (0, 2, 1)), entries, table.T]
    return kernel_call(
        functools.partial(warp_body, patches, visits, cap),
        [parcel] * (patches * visits),
        [HBM] * 5,
        [pltpu.SMEM(a.shape, a.dtype) for a in small]
        + [
            pltpu.VMEM(raw.shape, BF),
            pltpu.SemaphoreType.DMA((len(small),)),
            pltpu.SemaphoreType.DMA((math.gcd(4, tile_cols),)),
            pltpu.VMEM((patches * cap, side, side), BF),
            pltpu.VMEM((patches, LABELS, side), F32),
            pltpu.VMEM((2 * visit_count * tile_cols, side, side), BF),
        ],
        flops=4 * visit_count * tile_cols * side**3,
        data=4 * raw.size,
    )(*(pltpu.with_memory_space_constraint(a, pltpu.HBM) for a in (*small, raw)))


def tables_body(side, block, choice, coefs, listed, taps, heads, tails, plane, bands, mixes, ends):
    for j, t, b in itertools.product(*map(range, (*choice.shape, coefs.shape[0]))):
        row = (j * choice.shape[1] + t) * coefs.shape[0] + b
        mixes[row : row + 1, :] = jnp.full((1, side), coefs[b, choice[j, t]], F32)
    visit_total, tile_cols, per = listed.shape
    width = visit_total * per
    bad = jnp.concatenate([listed[v] for v in range(visit_total)], axis=1)
    bad_row = lax.div(bad, side)
    bad_col = bad - bad_row * side
    place = iota((side, width), 0)
    weight = (lax.div(iota((side, width), 1), per) + 1).astype(F32)
    for t in range(tile_cols):
        rows = jnp.where(bad_row[t : t + 1, :] == place, 1.0, 0.0).astype(BF)
        cols = jnp.where(bad_col[t : t + 1, :] == place, weight, 0.0).astype(BF)
        plane[:, t * side : (t + 1) * side] = lax.dot_general(
            rows, cols, (((1,), (1,)), ((), ())), preferred_element_type=F32
        )
    bases, pairs, lanes = taps.shape
    for b in range(bases):
        for j in range(pairs):
            rows = jnp.broadcast_to(taps[b, j : j + 1, :], (block, lanes))
            bands[b * block : (b + 1) * block, j * lanes : (j + 1) * lanes] = pltpu.roll(
                rows, 0, 1, stride=1, stride_axis=0
            ).astype(BF)
    margin = block // 2
    row, place = iota((block, lanes), 0), lax.rem(iota((block, lanes), 1), margin)
    for n, (source, shift, fits) in enumerate(
        ((heads, 0, place >= row), (tails, lanes - 2 * margin + 1, place <= row - margin))
    ):
        for b, j in itertools.product(range(bases), range(source.shape[1])):
            rows = jnp.broadcast_to(source[b, j : j + 1, :], (block, lanes))
            rolled = pltpu.roll(rows, shift, 1, stride=1, stride_axis=0)
            ends[n, b * block : (b + 1) * block, j * lanes : (j + 1) * lanes] = jnp.where(
                fits, rolled, 0.0
            ).astype(BF)


def make_tables(choice, coefs, listed, kernels, side, block):
    visit_total, tile_cols, per = listed.shape
    bases, taps, _ = kernels.shape
    window = block + taps - 1
    group = max(1, 128 // window)
    padded = -(-taps // group) * group
    turned = jnp.transpose(kernels, (0, 2, 1)).astype(F32)
    columns = jnp.pad(turned, ((0, 0), (0, padded - taps), (0, window - taps))).reshape(
        bases, padded // group, group * window
    )
    margin, lanes = taps // 2, group * window
    groups = -(-taps * margin // lanes)
    fill = ((0, 0), (0, groups * lanes // margin - taps), (0, 0))
    heads, tails = (
        jnp.pad(part, fill).reshape(bases, groups, lanes)
        for part in (turned[:, :, :margin], turned[:, :, margin + 1 :])
    )
    return kernel_call(
        functools.partial(tables_body, side, block),
        [
            jax.ShapeDtypeStruct((side, tile_cols * side), F32),
            jax.ShapeDtypeStruct((bases * block, padded * window), BF),
            jax.ShapeDtypeStruct((choice.size * bases, side), F32),
            jax.ShapeDtypeStruct((2, bases * block, groups * lanes), BF),
        ],
        [SMEM] * 2 + [VMEM] * 4,
        flops=2 * tile_cols * side * side * visit_total * per,
        data=4 * side * side * tile_cols,
    )(choice, coefs.T, listed, columns, heads, tails)


def place(parcels, cap, part, image, of):
    side = parcels[0].shape[1]
    tile_cols, dummy = image.shape[2] // side, image.shape[0] - 1
    for parcel in parcels:
        labels = parcel[cap * part :, :].astype(F32)
        for seat in range(cap):
            label = labels[seat, 0].astype(I32)
            number = lax.div(jnp.maximum(label, 0), tile_cols)
            column = jnp.where(label < 0, 0, label - number * tile_cols) * side
            which = jnp.where(label < 0, dummy, of(number))
            image[which, :, pl.ds(pl.multiple_of(column, side), side)] = parcel[
                seat * part : (seat + 1) * part, :
            ]


def land_body(visits, bands, visit_count, cap, plane, *refs):
    parcels, (slab, partial, image) = refs[:-3], refs[-3:]
    part = slab.shape[1]
    held = visits * visit_count
    visit, band = lax.axis_index("visit"), lax.axis_index("band")
    place(parcels, cap, part, image, lambda number: number)
    rows = pl.ds(pl.multiple_of(visit * part, part), part)
    side = parcels[0].shape[1]
    for start in range(0, image.shape[2], side):
        cols = slice(start, start + side)
        mine = plane[rows, cols]
        total = jnp.zeros(mine.shape, F32)
        high = jnp.full(mine.shape, -jnp.inf, F32)
        low = jnp.full(mine.shape, jnp.inf, F32)
        for n in range(held):
            own, local = divmod(n, visit_count)
            number = ((own * bands + band) * visit_count + local + 1).astype(F32)
            value = image[n, :, cols].astype(F32)
            bad = mine == number
            total = total + jnp.where(bad, 0.0, value)
            high = jnp.maximum(high, jnp.where(bad, -jnp.inf, value))
            low = jnp.minimum(low, jnp.where(bad, jnp.inf, value))
        partial[0, :, cols] = total.astype(BF)
        partial[1, :, cols] = high.astype(BF)
        partial[2, :, cols] = low.astype(BF)
    for j in range(visit_count):
        slab[j] = image[visit * visit_count + j]


def land_tiles(visits, bands, visit_count, cap, tile_cols, plane, parcels):
    side = parcels[0].shape[1]
    part = (parcels[0].shape[0] - LABELS) // cap
    width = tile_cols * side
    return kernel_call(
        functools.partial(land_body, visits, bands, visit_count, cap),
        [
            jax.ShapeDtypeStruct((visit_count, part, width), BF),
            jax.ShapeDtypeStruct((3, part, width), BF),
        ],
        [VMEM] * (1 + len(parcels)),
        [pltpu.VMEM((visits * visit_count + 1, part, width), BF)],
        flops=10 * visits * visit_count * part * width,
        data=4 * visits * visit_count * part * width,
    )(plane, *parcels)


def coadd_body(visit_total, margin, plane, *refs):
    partials, (coadd, share, edge) = refs[:-3], refs[-3:]
    part, some = coadd.shape[0], share.shape[0]
    visit, band = lax.axis_index("visit"), lax.axis_index("band")
    rows = pl.ds(pl.multiple_of(visit * part, part), part)
    width = coadd.shape[1]
    step = math.gcd(128, width)
    for first in range(0, width, step):
        cols = slice(first, first + step)
        total, high, low = (partials[0][n, :, cols].astype(F32) for n in range(3))
        for other in partials[1:]:
            total = total + other[0, :, cols].astype(F32)
            high = jnp.maximum(high, other[1, :, cols].astype(F32))
            low = jnp.minimum(low, other[2, :, cols].astype(F32))
        scale = jnp.where(
            plane[rows, cols] > 0.0, 1.0 / (visit_total - 3.0), 1.0 / (visit_total - 2.0)
        )
        coadd[:, cols] = ((total - high - low) * scale).astype(BF)
    share[...] = coadd[pl.ds(pl.multiple_of(band * some, some), some), :]
    start = pl.multiple_of(jnp.where(visit == 0, 0, part - margin), margin)
    edge[...] = coadd[pl.ds(start, margin), :]


def shifted(image, rows, margin, taps, side, first, until):
    width, height = image.shape[1], rows.stop - rows.start
    lane = iota((height, side), 1)
    blank = jnp.zeros((height, side), BF)
    shifts = []
    for dx in range(taps):
        shift = dx - margin
        low, high = (first - 1, until) if shift < 0 else (first, until + 1)
        turned = {
            t: pltpu.roll(image[rows, t * side : (t + 1) * side], -shift % side, 1)
            if 0 <= t < width // side
            else blank
            for t in range(low, high)
        } if shift else {}
        tiles = []
        for t in range(first, until):
            if shift < 0:
                tiles.append(jnp.where(lane < -shift, turned[t - 1], turned[t]))
            elif shift > 0:
                tiles.append(jnp.where(lane < side - shift, turned[t], turned[t + 1]))
            else:
                tiles.append(image[rows, t * side : (t + 1) * side])
        shifts.append(jnp.concatenate(tiles, axis=1))
    return shifts


def apply_rows(left, shifts, pick):
    right = jnp.concatenate([pick(dx, each) for dx, each in enumerate(shifts)], axis=0)
    return jnp.dot(left, right, preferred_element_type=F32)


def collect_body(visits, visit_count, cap, *refs):
    count = len(refs) - (visits - 1)
    parcels, others = refs[:count], refs[count:]
    each = count // (visits - 1)
    part = others[0].shape[1]
    for r, other in enumerate(others):
        place(
            parcels[r * each : (r + 1) * each],
            cap,
            part,
            other,
            lambda number: lax.rem(number, visit_count),
        )


def filter_ahead_body(margin, taps, side, per, low, bands, own, sums, edge):
    part, width = own.shape
    window = 2 * margin + taps - 1
    left = bands[:, : taps * window]
    rows = slice(0, window - margin) if low else slice(part - window + margin, part)
    outer = slice(0, margin) if low else slice(window - 2 * margin, window - margin)
    blank = jnp.zeros((margin, per * side), BF)
    for t in range(0, width // side, per):
        cols = slice(t * side, (t + per) * side)
        shifts = shifted(own, rows, margin, taps, side, t, t + per)
        sums[:, cols] = apply_rows(
            left, shifts, lambda dx, x: jnp.concatenate([blank, x] if low else [x, blank])
        )
        for dx, x in enumerate(shifts):
            edge[dx, :, cols] = x[outer]


def joined(pieces, halos, place_piece):
    sky, visit, band = (lax.axis_index(name) for name in ("sky", "visit", "band"))
    patches, visits = lax.axis_size("sky"), lax.axis_size("visit")
    for n, piece in enumerate(pieces):
        some = piece.shape[0]
        place_piece(lax.rem(visit + 1 + n // 2, visits), lax.rem(band + n, 2) * some, piece[...])
    mine = lax.rem(visit, 2) == band
    below = jnp.where(mine, halos[0][...], halos[1][...])
    above = jnp.where(mine, halos[1][...], halos[0][...])
    below = jnp.where(sky == patches - 1, jnp.zeros_like(below), below)
    above = jnp.where(sky == 0, jnp.zeros_like(above), above)
    return above, below


def render_body(
    margin, taps, tile_cols, per, bands, ends, mixes, plane, low, high, head, tail, slab, others, *refs
):
    width = plane.shape[1]
    pieces, halos, (out, result, sems, image) = refs[:-6], refs[-6:-4], refs[-4:]
    block, step = 2 * margin, per * (width // tile_cols)
    part = 2 * block
    window = block + taps - 1
    visit_count, side = result.shape[0], width // tile_cols
    bases = bands.shape[0] // block
    visit, band = lax.axis_index("visit"), lax.axis_index("band")
    band_count = lax.axis_size("band")
    first = visit == 0

    def put(_, start, piece):
        rows = pl.ds(pl.multiple_of(start, margin), piece.shape[0])
        image[rows, :] = piece

    above, below = joined(pieces, halos, put)
    image[part : part + margin, :] = above
    image[part + margin :, :] = below
    over, under = slice(part, part + margin), slice(part + margin, part + 2 * margin)
    top, bottom = slice(0, margin), slice(part - margin, part)
    numbers = [
        ((visit * band_count + band) * visit_count + j + 1).astype(F32)
        for j in range(visit_count)
    ]
    left = bands[:, : taps * window]

    def finish(start, n, c, source, value):
        value = value.astype(BF).astype(F32)
        rows = pl.ds(pl.multiple_of(start + n * block, block), block)
        for t in range(c * step // side, (c + 1) * step // side):
            cols = slice(t * side, (t + 1) * side)
            inset = slice(t * side - c * step, (t + 1) * side - c * step)
            planes = [value[b * block : (b + 1) * block, inset] for b in range(bases)]
            bad = plane[rows, cols]
            for j in range(visit_count):
                row = (j * tile_cols + t) * bases
                template = sum(mixes[row + b : row + b + 1, :] * planes[b] for b in range(bases))
                pixels = source[j, n * block : (n + 1) * block, cols].astype(F32) - template
                result[j, rows, cols] = jnp.where(bad == numbers[j], 0.0, pixels).astype(BF)

    copies = []
    for c in range(width // step):
        cols = slice(c * step, (c + 1) * step)
        shifts = shifted(image, slice(0, part + 2 * margin), margin, taps, side, c * per, (c + 1) * per)

        def upper(dx, x):
            before = jnp.where(first, tail[dx, :, cols], x[over])
            return jnp.concatenate([before, x[: window - margin]])

        def lower(dx, x):
            after = jnp.where(first, x[under], head[dx, :, cols])
            return jnp.concatenate([x[part - window + margin : part], after])

        start = (1 - visit) * part
        finish(start, 0, c, others, apply_rows(left, shifts, upper))
        finish(start, 1, c, others, apply_rows(left, shifts, lower))
        lack = apply_rows(
            ends[0, :, : taps * margin], shifts, lambda dx, x: jnp.where(first, x[over], x[bottom])
        )
        finish(visit * part, 0, c, slab, low[:, cols] + lack)
        lack = apply_rows(
            ends[1, :, : taps * margin], shifts, lambda dx, x: jnp.where(first, x[top], x[under])
        )
        finish(visit * part, 1, c, slab, high[:, cols] + lack)
        copies.append(
            pltpu.make_async_copy(result.at[:, :, cols], out.at[:, :, cols], sems.at[c])
        )
        copies[-1].start()
    for copy in copies:
        copy.wait()


def filter_body(margin, taps, side, per, bands, own, *refs):
    pieces, halos, (out, image) = refs[:-4], refs[-4:-2], refs[-2:]
    part, width = own.shape
    block = 2 * margin
    window = block + taps - 1

    def put(turn, start, piece):
        start = pl.multiple_of(turn * part + start + margin, margin)
        image[pl.ds(start, piece.shape[0])] = piece

    above, below = joined(pieces, halos, put)
    image[:margin] = above
    image[image.shape[0] - margin :] = below
    put(lax.axis_index("visit"), 0, own[...])
    for t in range(0, width // side, per):
        shifts = shifted(image, slice(0, image.shape[0]), margin, taps, side, t, t + per)
        for n in range(out.shape[0]):
            rows = slice(n * block, n * block + window)
            value = apply_rows(bands[:, : taps * window], shifts, lambda dx, x: x[rows])
            out[n, :, t * side : (t + per) * side] = value.astype(BF)


def finish_body(visits, bands, tile_cols, mixes, filtered, plane, *refs):
    slabs, (out, image, result, sems) = refs[:-4], refs[-4:]
    visit, band = lax.axis_index("visit"), lax.axis_index("band")
    part, width = slabs[0].shape[1:]
    visit_count = image.shape[0]
    blocks = filtered.shape[0]
    bases = mixes.shape[0] // (visit_count * tile_cols)
    block = filtered.shape[1] // bases
    side = width // tile_cols
    for r in range(visits):
        start = pl.multiple_of(lax.rem(visit + r, visits) * part, part)
        for j in range(visit_count):
            image[j, pl.ds(start, part), :] = slabs[r][j]
    numbers = [
        ((visit * bands + band) * visit_count + j + 1).astype(F32) for j in range(visit_count)
    ]
    copies = []
    for n in range(blocks):
        rows = slice(n * block, (n + 1) * block)
        for t in range(tile_cols):
            cols = slice(t * side, (t + 1) * side)
            planes = [
                filtered[n, b * block : (b + 1) * block, cols].astype(F32) for b in range(bases)
            ]
            bad = plane[rows, cols]
            for j in range(visit_count):
                row = (j * tile_cols + t) * bases
                template = sum(mixes[row + b : row + b + 1, :] * planes[b] for b in range(bases))
                value = image[j, rows, cols].astype(F32) - template
                result[j, rows, cols] = jnp.where(bad == numbers[j], 0.0, value).astype(BF)
        copies.append(pltpu.make_async_copy(result.at[:, rows], out.at[:, rows], sems.at[n]))
        copies[-1].start()
    for copy in copies:
        copy.wait()


def on_device(
    raw_tiles,
    pixel_offsets,
    shift_entry_index,
    shift_table,
    tile_routes,
    bad_pixels,
    basis_kernels,
    basis_choice,
    coef_table,
):
    visit_count, tile_cols, side = raw_tiles.shape[:3]
    patches, visits, bands = (lax.axis_size(name) for name in ("sky", "visit", "band"))
    cap = (visit_count * tile_cols + patches - 1) // patches + 1
    part, width = side // visits, tile_cols * side
    visit_total = bad_pixels.shape[0]
    bases, taps = basis_kernels.shape[:2]
    margin = taps // 2
    block = 2 * margin

    parcels = warp_tiles(
        patches, visits, cap, raw_tiles, pixel_offsets, shift_entry_index, shift_table, tile_routes
    )
    far = sorted(range(patches), key=lambda k: (-min(k, patches - k), -k))
    order = [k * visits + r for r in reversed(range(visits)) for k in far if k + r > 0]
    arrived = {0: parcels[0]}
    for n in order:
        k, r = divmod(n, visits)
        pairs = [
            (s * visits + v, (s + k) % patches * visits + (v + r) % visits)
            for s in range(patches)
            for v in range(visits)
        ]
        arrived[n] = lax.ppermute(parcels[n], ("sky", "visit"), pairs)
    own_others = []
    for r in range(1, visits):
        own_others.append(parcels[r])
        for k in (k for k in far if k > 0):
            own_others.append(
                lax.ppermute(
                    arrived[k * visits + r], "visit", [(v, (v - r) % visits) for v in range(visits)]
                )
            )
    plane, toeplitz, mixes, ends = make_tables(
        basis_choice, coef_table, bad_pixels, basis_kernels, side, block
    )
    slab, partial = land_tiles(
        visits, bands, visit_count, cap, tile_cols, plane, list(arrived.values())
    )

    partials = [partial] + [
        lax.ppermute(partial, "band", [(b, (b + q) % bands) for b in range(bands)])
        for q in range(1, bands)
    ]
    coadd, share, edge = kernel_call(
        functools.partial(coadd_body, visit_total, margin),
        [jax.ShapeDtypeStruct((rows, width), BF) for rows in (part, part // bands, margin)],
        [VMEM] * (1 + bands),
        flops=8 * part * width,
        data=8 * part * width,
    )(plane, *partials)

    def turn(r):
        return [(v, (v - r) % visits) for v in range(visits)]

    swap = [(b, (b + 1) % bands) for b in range(bands)]
    pieces = []
    for r in range(1, visits):
        pieces.append(lax.ppermute(share, "visit", turn(r)))
        pieces.append(lax.ppermute(pieces[-1], "band", swap))
    halos = []
    for first in range(0, visits, bands):
        pairs = []
        for s, b in itertools.product(range(patches), range(bands)):
            r = first + b
            top = ((s - 1) % patches, r)
            bottom = ((s + 1) % patches, visits - 1 - r)
            for v, (to_s, to_v) in ((0, top), (visits - 1, bottom)):
                pairs.append(((s * visits + v) * bands + b, (to_s * visits + to_v) * bands + b))
        halos.append(lax.ppermute(edge, ("sky", "visit", "band"), pairs))
    halo = functools.reduce(jnp.add, halos)
    halos = [halo, lax.ppermute(halo, "band", swap)]
    others = kernel_call(
        functools.partial(collect_body, visits, visit_count, cap),
        [jax.ShapeDtypeStruct((visit_count + 1, part, width), BF)] * (visits - 1),
        [VMEM] * len(own_others),
        flops=part * width,
        data=4 * visit_count * side * width,
    )(*own_others)
    work = 2 * bases * side * width * taps * (block + taps - 1)
    per = tile_cols
    result = jax.ShapeDtypeStruct((visit_count, side, width), BF)
    if visits == 2 and part == 2 * block:
        sums, edges = [], []
        for low in (True, False):
            one, edge = kernel_call(
                functools.partial(filter_ahead_body, margin, taps, side, per, low),
                [
                    jax.ShapeDtypeStruct((bases * block, width), F32),
                    jax.ShapeDtypeStruct((taps, margin, width), BF),
                ],
                [VMEM] * 2,
                flops=work // 4,
                data=4 * bases * part * width,
                spare=16,
            )(toeplitz, coadd)
            sums.append(one)
            edges.append(edge)
        return kernel_call(
            functools.partial(render_body, margin, taps, tile_cols, per),
            result,
            [VMEM] * (10 + len(pieces) + 2),
            [
                pltpu.VMEM(result.shape, BF),
                pltpu.SemaphoreType.DMA((tile_cols // per,)),
                pltpu.VMEM((part + 2 * margin, width), BF),
            ],
            flops=work // 2,
            data=2 * bases * side * width,
            spare=24,
            out_specs=HBM,
        )(toeplitz, ends, mixes, plane, *sums, *edges, slab, *others, *pieces, *halos)
    filtered = kernel_call(
        functools.partial(filter_body, margin, taps, side, per),
        jax.ShapeDtypeStruct((side // block, bases * block, width), BF),
        [VMEM] * (2 + len(pieces) + 2),
        [pltpu.VMEM((side + 2 * margin, width), BF)],
        flops=work,
        data=2 * bases * side * width,
        spare=24,
    )(toeplitz, coadd, *pieces, *halos)
    return kernel_call(
        functools.partial(finish_body, visits, bands, tile_cols),
        result,
        [VMEM] * (3 + visits),
        [
            pltpu.VMEM(result.shape, BF),
            pltpu.VMEM(result.shape, BF),
            pltpu.SemaphoreType.DMA((side // block,)),
        ],
        flops=20 * visit_count * side * width,
        data=4 * visit_count * side * width,
        out_specs=HBM,
    )(mixes, filtered, plane, slab, *others)


def solution(mesh):
    return jax.shard_map(
        on_device,
        mesh=mesh,
        in_specs=(
            P(("group", "visit", "band"), "sky", None, None),
            P(("group", "visit", "band"), "sky", None),
            P(("group", "visit", "band"), "sky"),
            P(),
            P(("group", "visit", "band"), "sky"),
            P("group", "sky", None),
            P(),
            P(("group", "visit", "band"), "sky"),
            P(),
        ),
        out_specs=P(("group", "visit", "band"), "sky", None),
        check_vma=False,
    )
```

```python
import functools
import itertools
import math

import jax
import jax.numpy as jnp
from jax import lax
from jax.experimental import pallas as pl
from jax.experimental.pallas import tpu as pltpu
from jax.sharding import PartitionSpec as P


BF = jnp.bfloat16
F32 = jnp.float32
I32 = jnp.int32
VMEM = pl.BlockSpec(memory_space=pltpu.VMEM)
SMEM = pl.BlockSpec(memory_space=pltpu.SMEM)
HBM = pl.BlockSpec(memory_space=pltpu.HBM)
LABELS = 8


def kernel_call(body, outs, in_specs, scratch=(), flops=0, data=0, out_specs=None, spare=4):
    def call(*args):
        held = [*args, *jax.tree.leaves(outs), *(s for s in scratch if len(s.shape) > 1)]
        places = out_specs or jax.tree.map(lambda _: VMEM, outs)
        room = sum(math.prod(a.shape) * jnp.dtype(a.dtype).itemsize for a in held)
        return pl.pallas_call(
            body,
            out_shape=outs,
            in_specs=in_specs,
            out_specs=places,
            scratch_shapes=list(scratch),
            cost_estimate=pl.CostEstimate(flops=flops, bytes_accessed=data, transcendentals=0),
            compiler_params=pltpu.CompilerParams(vmem_limit_bytes=room + room // 4 + (spare << 20)),
        )(*args)

    return call


def sinc(x):
    angle = x * jnp.float32(jnp.pi)
    safe = jnp.where(x == 0.0, 1.0, angle)
    return jnp.where(x == 0.0, 1.0, jnp.sin(safe) / safe)


def iota(shape, dim):
    return lax.broadcasted_iota(I32, shape, dim)


def warp_body(patches, visits, cap, *refs):
    sources, parcels, held = refs[:5], refs[5:-9], refs[-9:]
    routes, offsets, entries, table, raw, small, large, seats, labels = held
    copies = [
        pltpu.make_async_copy(source, target, small.at[n])
        for n, (source, target) in enumerate(zip(sources[:4], held[:4]))
    ]
    groups = large.shape[0]
    per_group = raw.shape[1] // groups
    loads = [
        pltpu.make_async_copy(
            sources[4].at[:, g * per_group : (g + 1) * per_group],
            raw.at[:, g * per_group : (g + 1) * per_group],
            large.at[g],
        )
        for g in range(groups)
    ]
    for copy in copies + loads:
        copy.start()
    visit_count, tile_cols, side, _ = raw.shape
    tiles = visit_count * tile_cols
    part = side // visits
    sky, visit = lax.axis_index("sky"), lax.axis_index("visit")
    for copy in copies:
        copy.wait()
    row = iota((2 * tiles, side), 0)
    shift = jnp.zeros((2 * tiles, side), F32)
    for n in range(tiles):
        v, i = divmod(n, tile_cols)
        entry = entries[v, i]
        for axis in range(2):
            amount = offsets[v, axis, i].astype(F32) + table[axis, entry]
            shift = jnp.where(row == 2 * n + axis, amount, shift)
    lane = iota((2 * tiles, side), 1)
    step = jnp.where(lane < side // 2, lane, lane - side)
    x = jnp.where(row % 2 == 0, -step, step).astype(F32) - shift
    taps = jnp.where(jnp.abs(x) < 3.0, sinc(x) * sinc(x / 3.0), 0.0)
    near = jnp.abs(iota((side, side), 1) - iota((side, side), 0)) < side // 2

    def spread(index):
        rows = jnp.broadcast_to(taps[index : index + 1, :], (side, side))
        rolled = pltpu.roll(rows, 0, 1, stride=1, stride_axis=0)
        return jnp.where(near, rolled, 0.0).astype(BF)

    for load in loads:
        load.wait()
    for k in range(patches):
        labels[k] = jnp.full((LABELS, side), -1.0, F32)
    count = [jnp.int32(0)] * patches
    for i, v in itertools.product(range(tile_cols), range(visit_count)):
        n = v * tile_cols + i
        halfway = jnp.dot(spread(2 * n), raw[v, i], preferred_element_type=F32).astype(BF)
        warped = jnp.dot(halfway, spread(2 * n + 1), preferred_element_type=F32).astype(BF)
        route = routes[v, i]
        owner = lax.div(route, tile_cols)
        slot = route - owner * tile_cols
        relative = lax.rem(owner - sky + patches, patches)
        seat = sum(jnp.where(relative == k, count[k], 0) for k in range(patches))
        count = [count[k] + (relative == k).astype(I32) for k in range(patches)]
        seats[relative * cap + seat] = warped
        labels[relative, pl.ds(seat, 1), :] = jnp.full(
            (1, side), ((visit * visit_count + v) * tile_cols + slot).astype(F32), F32
        )
    for k in range(patches):
        for r in range(visits):
            parcel = parcels[k * visits + r]
            target = lax.rem(visit + r, visits)
            rows = pl.ds(pl.multiple_of(target * part, part), part)
            for seat in range(cap):
                parcel[seat * part : (seat + 1) * part, :] = seats[k * cap + seat, rows, :]
            parcel[cap * part :, :] = labels[k].astype(BF)


def warp_tiles(patches, visits, cap, raw, offsets, entries, table, routes):
    visit_count, tile_cols, side, _ = raw.shape
    parcel = jax.ShapeDtypeStruct((cap * (side // visits) + LABELS, side), BF)
    small = [routes, jnp.transpose(offsets, (0, 2, 1)), entries, table.T]
    return kernel_call(
        functools.partial(warp_body, patches, visits, cap),
        [parcel] * (patches * visits),
        [HBM] * 5,
        [pltpu.SMEM(a.shape, a.dtype) for a in small]
        + [
            pltpu.VMEM(raw.shape, BF),
            pltpu.SemaphoreType.DMA((len(small),)),
            pltpu.SemaphoreType.DMA((math.gcd(4, tile_cols),)),
            pltpu.VMEM((patches * cap, side, side), BF),
            pltpu.VMEM((patches, LABELS, side), F32),
        ],
        flops=4 * visit_count * tile_cols * side**3,
        data=4 * raw.size,
    )(*(pltpu.with_memory_space_constraint(a, pltpu.HBM) for a in (*small, raw)))


def tables_body(side, block, choice, coefs, listed, taps, heads, tails, plane, bands, mixes, ends):
    for j, t, b in itertools.product(*map(range, (*choice.shape, coefs.shape[0]))):
        row = (j * choice.shape[1] + t) * coefs.shape[0] + b
        mixes[row : row + 1, :] = jnp.full((1, side), coefs[b, choice[j, t]], F32)
    visit_total, tile_cols, per = listed.shape
    width = visit_total * per
    bad = jnp.concatenate([listed[v] for v in range(visit_total)], axis=1)
    bad_row = lax.div(bad, side)
    bad_col = bad - bad_row * side
    place = iota((side, width), 0)
    weight = (lax.div(iota((side, width), 1), per) + 1).astype(F32)
    for t in range(tile_cols):
        rows = jnp.where(bad_row[t : t + 1, :] == place, 1.0, 0.0).astype(BF)
        cols = jnp.where(bad_col[t : t + 1, :] == place, weight, 0.0).astype(BF)
        plane[:, t * side : (t + 1) * side] = lax.dot_general(
            rows, cols, (((1,), (1,)), ((), ())), preferred_element_type=F32
        )
    bases, pairs, lanes = taps.shape
    for b in range(bases):
        for j in range(pairs):
            rows = jnp.broadcast_to(taps[b, j : j + 1, :], (block, lanes))
            bands[b * block : (b + 1) * block, j * lanes : (j + 1) * lanes] = pltpu.roll(
                rows, 0, 1, stride=1, stride_axis=0
            ).astype(BF)
    margin = block // 2
    row, place = iota((block, lanes), 0), lax.rem(iota((block, lanes), 1), margin)
    for n, (source, shift, fits) in enumerate(
        ((heads, 0, place >= row), (tails, lanes - 2 * margin + 1, place <= row - margin))
    ):
        for b, j in itertools.product(range(bases), range(source.shape[1])):
            rows = jnp.broadcast_to(source[b, j : j + 1, :], (block, lanes))
            rolled = pltpu.roll(rows, shift, 1, stride=1, stride_axis=0)
            ends[n, b * block : (b + 1) * block, j * lanes : (j + 1) * lanes] = jnp.where(
                fits, rolled, 0.0
            ).astype(BF)


def make_tables(choice, coefs, listed, kernels, side, block):
    visit_total, tile_cols, per = listed.shape
    bases, taps, _ = kernels.shape
    window = block + taps - 1
    group = max(1, 128 // window)
    padded = -(-taps // group) * group
    turned = jnp.transpose(kernels, (0, 2, 1)).astype(F32)
    columns = jnp.pad(turned, ((0, 0), (0, padded - taps), (0, window - taps))).reshape(
        bases, padded // group, group * window
    )
    margin, lanes = taps // 2, group * window
    groups = -(-taps * margin // lanes)
    fill = ((0, 0), (0, groups * lanes // margin - taps), (0, 0))
    heads, tails = (
        jnp.pad(part, fill).reshape(bases, groups, lanes)
        for part in (turned[:, :, :margin], turned[:, :, margin + 1 :])
    )
    return kernel_call(
        functools.partial(tables_body, side, block),
        [
            jax.ShapeDtypeStruct((side, tile_cols * side), F32),
            jax.ShapeDtypeStruct((bases * block, padded * window), BF),
            jax.ShapeDtypeStruct((choice.size * bases, side), F32),
            jax.ShapeDtypeStruct((2, bases * block, groups * lanes), BF),
        ],
        [SMEM] * 2 + [VMEM] * 4,
        flops=2 * tile_cols * side * side * visit_total * per,
        data=4 * side * side * tile_cols,
    )(choice, coefs.T, listed, columns, heads, tails)


def place(parcels, cap, part, image, of):
    side = parcels[0].shape[1]
    tile_cols, dummy = image.shape[2] // side, image.shape[0] - 1
    for parcel in parcels:
        labels = parcel[cap * part :, :].astype(F32)
        for seat in range(cap):
            label = labels[seat, 0].astype(I32)
            number = lax.div(jnp.maximum(label, 0), tile_cols)
            column = jnp.where(label < 0, 0, label - number * tile_cols) * side
            which = jnp.where(label < 0, dummy, of(number))
            image[which, :, pl.ds(pl.multiple_of(column, side), side)] = parcel[
                seat * part : (seat + 1) * part, :
            ]


def land_body(visits, bands, visit_count, cap, plane, *refs):
    parcels, (slab, partial, image) = refs[:-3], refs[-3:]
    part = slab.shape[1]
    held = visits * visit_count
    visit, band = lax.axis_index("visit"), lax.axis_index("band")
    place(parcels, cap, part, image, lambda number: number)
    rows = pl.ds(pl.multiple_of(visit * part, part), part)
    side = parcels[0].shape[1]
    for start in range(0, image.shape[2], side):
        cols = slice(start, start + side)
        mine = plane[rows, cols]
        total = jnp.zeros(mine.shape, F32)
        high = jnp.full(mine.shape, -jnp.inf, F32)
        low = jnp.full(mine.shape, jnp.inf, F32)
        for n in range(held):
            own, local = divmod(n, visit_count)
            number = ((own * bands + band) * visit_count + local + 1).astype(F32)
            value = image[n, :, cols].astype(F32)
            bad = mine == number
            total = total + jnp.where(bad, 0.0, value)
            high = jnp.maximum(high, jnp.where(bad, -jnp.inf, value))
            low = jnp.minimum(low, jnp.where(bad, jnp.inf, value))
        partial[0, :, cols] = total.astype(BF)
        partial[1, :, cols] = high.astype(BF)
        partial[2, :, cols] = low.astype(BF)
    for j in range(visit_count):
        slab[j] = image[visit * visit_count + j]


def land_tiles(visits, bands, visit_count, cap, tile_cols, plane, parcels):
    side = parcels[0].shape[1]
    part = (parcels[0].shape[0] - LABELS) // cap
    width = tile_cols * side
    return kernel_call(
        functools.partial(land_body, visits, bands, visit_count, cap),
        [
            jax.ShapeDtypeStruct((visit_count, part, width), BF),
            jax.ShapeDtypeStruct((3, part, width), BF),
        ],
        [VMEM] * (1 + len(parcels)),
        [pltpu.VMEM((visits * visit_count + 1, part, width), BF)],
        flops=10 * visits * visit_count * part * width,
        data=4 * visits * visit_count * part * width,
    )(plane, *parcels)


def coadd_body(visit_total, margin, plane, *refs):
    partials, (coadd, edge) = refs[:-2], refs[-2:]
    part = coadd.shape[0]
    visit = lax.axis_index("visit")
    rows = pl.ds(pl.multiple_of(visit * part, part), part)
    width = coadd.shape[1]
    step = math.gcd(128, width)
    for first in range(0, width, step):
        cols = slice(first, first + step)
        total, high, low = (partials[0][n, :, cols].astype(F32) for n in range(3))
        for other in partials[1:]:
            total = total + other[0, :, cols].astype(F32)
            high = jnp.maximum(high, other[1, :, cols].astype(F32))
            low = jnp.minimum(low, other[2, :, cols].astype(F32))
        scale = jnp.where(
            plane[rows, cols] > 0.0, 1.0 / (visit_total - 3.0), 1.0 / (visit_total - 2.0)
        )
        coadd[:, cols] = ((total - high - low) * scale).astype(BF)
    start = pl.multiple_of(jnp.where(visit == 0, 0, part - margin), margin)
    edge[...] = coadd[pl.ds(start, margin), :]


def shifted(image, rows, margin, taps, side, first, until, made):
    width, height = image.shape[1], rows.stop - rows.start
    lane = iota((height, side), 1)
    blank = jnp.zeros((height, side), BF)
    shifts = []
    for dx in range(taps):
        shift = dx - margin
        low, high = (first - 1, until) if shift < 0 else (first, until + 1)
        for t in range(low, high) if shift else ():
            if not 0 <= t < width // side:
                made[t, dx] = blank
            elif (t, dx) not in made:
                made[t, dx] = pltpu.roll(image[rows, t * side : (t + 1) * side], -shift % side, 1)
        tiles = []
        for t in range(first, until):
            if shift < 0:
                tiles.append(jnp.where(lane < -shift, made[t - 1, dx], made[t, dx]))
            elif shift > 0:
                tiles.append(jnp.where(lane < side - shift, made[t, dx], made[t + 1, dx]))
            else:
                tiles.append(image[rows, t * side : (t + 1) * side])
        shifts.append(jnp.concatenate(tiles, axis=1))
    return shifts


def apply_rows(left, shifts, pick):
    right = jnp.concatenate([pick(dx, each) for dx, each in enumerate(shifts)], axis=0)
    return jnp.dot(left, right, preferred_element_type=F32)


def collect_body(visits, visit_count, cap, *refs):
    count = len(refs) - (visits - 1)
    parcels, others = refs[:count], refs[count:]
    each = count // (visits - 1)
    part = others[0].shape[1]
    for r, other in enumerate(others):
        place(
            parcels[r * each : (r + 1) * each],
            cap,
            part,
            other,
            lambda number: lax.rem(number, visit_count),
        )


def filter_ahead_body(margin, taps, side, per, low, bands, own, sums, edge):
    part, width = own.shape
    window = 2 * margin + taps - 1
    left = bands[:, : taps * window]
    rows = slice(0, window - margin) if low else slice(part - window + margin, part)
    outer = slice(0, margin) if low else slice(window - 2 * margin, window - margin)
    blank = jnp.zeros((margin, per * side), BF)
    made = {}
    for t in range(0, width // side, per):
        cols = slice(t * side, (t + per) * side)
        shifts = shifted(own, rows, margin, taps, side, t, t + per, made)
        sums[:, cols] = apply_rows(
            left, shifts, lambda dx, x: jnp.concatenate([blank, x] if low else [x, blank])
        )
        for dx, x in enumerate(shifts):
            edge[dx, :, cols] = x[outer]


def joined(pieces, halos, place_piece):
    sky, visit, band = (lax.axis_index(name) for name in ("sky", "visit", "band"))
    patches, visits = lax.axis_size("sky"), lax.axis_size("visit")
    for n, piece in enumerate(pieces):
        place_piece(lax.rem(visit + 1 + n, visits), piece[...])
    mine = lax.rem(visit, 2) == band
    below = jnp.where(mine, halos[0][...], halos[1][...])
    above = jnp.where(mine, halos[1][...], halos[0][...])
    below = jnp.where(sky == patches - 1, jnp.zeros_like(below), below)
    above = jnp.where(sky == 0, jnp.zeros_like(above), above)
    return above, below


def render_body(
    margin, taps, tile_cols, per, bands, ends, mixes, plane, low, high, head, tail, slab, others, *refs
):
    width = plane.shape[1]
    pieces, halos, (out, result, sems, image) = refs[:-6], refs[-6:-4], refs[-4:]
    block, step = 2 * margin, per * (width // tile_cols)
    part = 2 * block
    window = block + taps - 1
    visit_count, side = result.shape[0], width // tile_cols
    bases = bands.shape[0] // block
    visit, band = lax.axis_index("visit"), lax.axis_index("band")
    band_count = lax.axis_size("band")
    first = visit == 0

    def put(_, piece):
        image[:part, :] = piece

    above, below = joined(pieces, halos, put)
    image[part : part + margin, :] = above
    image[part + margin :, :] = below
    over, under = slice(part, part + margin), slice(part + margin, part + 2 * margin)
    top, bottom = slice(0, margin), slice(part - margin, part)
    numbers = [
        ((visit * band_count + band) * visit_count + j + 1).astype(F32)
        for j in range(visit_count)
    ]
    left = bands[:, : taps * window]

    def finish(start, n, c, source, value):
        value = value.astype(BF).astype(F32)
        rows = pl.ds(pl.multiple_of(start + n * block, block), block)
        for t in range(c * step // side, (c + 1) * step // side):
            cols = slice(t * side, (t + 1) * side)
            inset = slice(t * side - c * step, (t + 1) * side - c * step)
            planes = [value[b * block : (b + 1) * block, inset] for b in range(bases)]
            bad = plane[rows, cols]
            for j in range(visit_count):
                row = (j * tile_cols + t) * bases
                template = sum(mixes[row + b : row + b + 1, :] * planes[b] for b in range(bases))
                pixels = source[j, n * block : (n + 1) * block, cols].astype(F32) - template
                result[j, rows, cols] = jnp.where(bad == numbers[j], 0.0, pixels).astype(BF)

    copies = []
    made = {}
    for c in range(width // step):
        cols = slice(c * step, (c + 1) * step)
        shifts = shifted(image, slice(0, part + 2 * margin), margin, taps, side, c * per, (c + 1) * per, made)

        def upper(dx, x):
            before = jnp.where(first, tail[dx, :, cols], x[over])
            return jnp.concatenate([before, x[: window - margin]])

        def lower(dx, x):
            after = jnp.where(first, x[under], head[dx, :, cols])
            return jnp.concatenate([x[part - window + margin : part], after])

        start = (1 - visit) * part
        finish(start, 0, c, others, apply_rows(left, shifts, upper))
        finish(start, 1, c, others, apply_rows(left, shifts, lower))
        lack = apply_rows(
            ends[0, :, : taps * margin], shifts, lambda dx, x: jnp.where(first, x[over], x[bottom])
        )
        finish(visit * part, 0, c, slab, low[:, cols] + lack)
        lack = apply_rows(
            ends[1, :, : taps * margin], shifts, lambda dx, x: jnp.where(first, x[top], x[under])
        )
        finish(visit * part, 1, c, slab, high[:, cols] + lack)
        copies.append(
            pltpu.make_async_copy(result.at[:, :, cols], out.at[:, :, cols], sems.at[c])
        )
        copies[-1].start()
    for copy in copies:
        copy.wait()


def filter_body(margin, taps, side, per, bands, own, *refs):
    pieces, halos, (out, image) = refs[:-4], refs[-4:-2], refs[-2:]
    part, width = own.shape
    block = 2 * margin
    window = block + taps - 1

    def put(turn, piece):
        image[pl.ds(pl.multiple_of(turn * part + margin, margin), part), :] = piece

    above, below = joined(pieces, halos, put)
    image[:margin] = above
    image[image.shape[0] - margin :] = below
    put(lax.axis_index("visit"), own[...])
    made = {}
    for t in range(0, width // side, per):
        shifts = shifted(image, slice(0, image.shape[0]), margin, taps, side, t, t + per, made)
        for n in range(out.shape[0]):
            rows = slice(n * block, n * block + window)
            value = apply_rows(bands[:, : taps * window], shifts, lambda dx, x: x[rows])
            out[n, :, t * side : (t + per) * side] = value.astype(BF)


def finish_body(visits, bands, tile_cols, mixes, filtered, plane, *refs):
    slabs, (out, image, result, sems) = refs[:-4], refs[-4:]
    visit, band = lax.axis_index("visit"), lax.axis_index("band")
    part, width = slabs[0].shape[1:]
    visit_count = image.shape[0]
    blocks = filtered.shape[0]
    bases = mixes.shape[0] // (visit_count * tile_cols)
    block = filtered.shape[1] // bases
    side = width // tile_cols
    for r in range(visits):
        start = pl.multiple_of(lax.rem(visit + r, visits) * part, part)
        for j in range(visit_count):
            image[j, pl.ds(start, part), :] = slabs[r][j]
    numbers = [
        ((visit * bands + band) * visit_count + j + 1).astype(F32) for j in range(visit_count)
    ]
    copies = []
    for n in range(blocks):
        rows = slice(n * block, (n + 1) * block)
        for t in range(tile_cols):
            cols = slice(t * side, (t + 1) * side)
            planes = [
                filtered[n, b * block : (b + 1) * block, cols].astype(F32) for b in range(bases)
            ]
            bad = plane[rows, cols]
            for j in range(visit_count):
                row = (j * tile_cols + t) * bases
                template = sum(mixes[row + b : row + b + 1, :] * planes[b] for b in range(bases))
                value = image[j, rows, cols].astype(F32) - template
                result[j, rows, cols] = jnp.where(bad == numbers[j], 0.0, value).astype(BF)
        copies.append(pltpu.make_async_copy(result.at[:, rows], out.at[:, rows], sems.at[n]))
        copies[-1].start()
    for copy in copies:
        copy.wait()


def on_device(
    raw_tiles,
    pixel_offsets,
    shift_entry_index,
    shift_table,
    tile_routes,
    bad_pixels,
    basis_kernels,
    basis_choice,
    coef_table,
):
    visit_count, tile_cols, side = raw_tiles.shape[:3]
    patches, visits, bands = (lax.axis_size(name) for name in ("sky", "visit", "band"))
    cap = (visit_count * tile_cols + patches - 1) // patches + 1
    part, width = side // visits, tile_cols * side
    visit_total = bad_pixels.shape[0]
    bases, taps = basis_kernels.shape[:2]
    margin = taps // 2
    block = 2 * margin

    parcels = warp_tiles(
        patches, visits, cap, raw_tiles, pixel_offsets, shift_entry_index, shift_table, tile_routes
    )
    far = sorted(range(patches), key=lambda k: (-min(k, patches - k), -k))
    order = [k * visits + r for r in reversed(range(visits)) for k in far if k + r > 0]
    arrived = {0: parcels[0]}
    for n in order:
        k, r = divmod(n, visits)
        pairs = [
            (s * visits + v, (s + k) % patches * visits + (v + r) % visits)
            for s in range(patches)
            for v in range(visits)
        ]
        arrived[n] = lax.ppermute(parcels[n], ("sky", "visit"), pairs)
    own_others = []
    for r in range(1, visits):
        own_others.append(parcels[r])
        for k in (k for k in far if k > 0):
            own_others.append(
                lax.ppermute(
                    arrived[k * visits + r], "visit", [(v, (v - r) % visits) for v in range(visits)]
                )
            )
    plane, toeplitz, mixes, ends = make_tables(
        basis_choice, coef_table, bad_pixels, basis_kernels, side, block
    )
    slab, partial = land_tiles(
        visits, bands, visit_count, cap, tile_cols, plane, list(arrived.values())
    )

    partials = [partial] + [
        lax.ppermute(partial, "band", [(b, (b + q) % bands) for b in range(bands)])
        for q in range(1, bands)
    ]
    coadd, edge = kernel_call(
        functools.partial(coadd_body, visit_total, margin),
        [jax.ShapeDtypeStruct((rows, width), BF) for rows in (part, margin)],
        [VMEM] * (1 + bands),
        flops=8 * part * width,
        data=8 * part * width,
    )(plane, *partials)

    def turn(r):
        return [(v, (v - r) % visits) for v in range(visits)]

    swap = [(b, (b + 1) % bands) for b in range(bands)]
    pieces = []
    for r in range(1, visits):
        pieces.append(lax.ppermute(coadd, "visit", turn(r)))
    halos = []
    for first in range(0, visits, bands):
        pairs = []
        for s, b in itertools.product(range(patches), range(bands)):
            r = first + b
            top = ((s - 1) % patches, r)
            bottom = ((s + 1) % patches, visits - 1 - r)
            for v, (to_s, to_v) in ((0, top), (visits - 1, bottom)):
                pairs.append(((s * visits + v) * bands + b, (to_s * visits + to_v) * bands + b))
        halos.append(lax.ppermute(edge, ("sky", "visit", "band"), pairs))
    halo = functools.reduce(jnp.add, halos)
    halos = [halo, lax.ppermute(halo, "band", swap)]
    others = kernel_call(
        functools.partial(collect_body, visits, visit_count, cap),
        [jax.ShapeDtypeStruct((visit_count + 1, part, width), BF)] * (visits - 1),
        [VMEM] * len(own_others),
        flops=part * width,
        data=4 * visit_count * side * width,
    )(*own_others)
    work = 2 * bases * side * width * taps * (block + taps - 1)
    per = math.gcd(4, tile_cols)
    result = jax.ShapeDtypeStruct((visit_count, side, width), BF)
    if visits == 2 and part == 2 * block:
        sums, edges = [], []
        for low in (True, False):
            one, edge = kernel_call(
                functools.partial(filter_ahead_body, margin, taps, side, per, low),
                [
                    jax.ShapeDtypeStruct((bases * block, width), F32),
                    jax.ShapeDtypeStruct((taps, margin, width), BF),
                ],
                [VMEM] * 2,
                flops=work // 4,
                data=4 * bases * part * width,
                spare=16,
            )(toeplitz, coadd)
            sums.append(one)
            edges.append(edge)
        return kernel_call(
            functools.partial(render_body, margin, taps, tile_cols, per),
            result,
            [VMEM] * (10 + len(pieces) + 2),
            [
                pltpu.VMEM(result.shape, BF),
                pltpu.SemaphoreType.DMA((tile_cols // per,)),
                pltpu.VMEM((part + 2 * margin, width), BF),
            ],
            flops=work // 2,
            data=2 * bases * side * width,
            spare=24,
            out_specs=HBM,
        )(toeplitz, ends, mixes, plane, *sums, *edges, slab, *others, *pieces, *halos)
    filtered = kernel_call(
        functools.partial(filter_body, margin, taps, side, per),
        jax.ShapeDtypeStruct((side // block, bases * block, width), BF),
        [VMEM] * (2 + len(pieces) + 2),
        [pltpu.VMEM((side + 2 * margin, width), BF)],
        flops=work,
        data=2 * bases * side * width,
        spare=24,
    )(toeplitz, coadd, *pieces, *halos)
    return kernel_call(
        functools.partial(finish_body, visits, bands, tile_cols),
        result,
        [VMEM] * (3 + visits),
        [
            pltpu.VMEM(result.shape, BF),
            pltpu.VMEM(result.shape, BF),
            pltpu.SemaphoreType.DMA((side // block,)),
        ],
        flops=20 * visit_count * side * width,
        data=4 * visit_count * side * width,
        out_specs=HBM,
    )(mixes, filtered, plane, slab, *others)


def solution(mesh):
    return jax.shard_map(
        on_device,
        mesh=mesh,
        in_specs=(
            P(("group", "visit", "band"), "sky", None, None),
            P(("group", "visit", "band"), "sky", None),
            P(("group", "visit", "band"), "sky"),
            P(),
            P(("group", "visit", "band"), "sky"),
            P("group", "sky", None),
            P(),
            P(("group", "visit", "band"), "sky"),
            P(),
        ),
        out_specs=P(("group", "visit", "band"), "sky", None),
        check_vma=False,
    )
```

```python
import functools
import itertools
import math

import jax
import jax.numpy as jnp
from jax import lax
from jax.experimental import pallas as pl
from jax.experimental.pallas import tpu as pltpu
from jax.sharding import PartitionSpec as P


BF = jnp.bfloat16
F32 = jnp.float32
I32 = jnp.int32
VMEM = pl.BlockSpec(memory_space=pltpu.VMEM)
SMEM = pl.BlockSpec(memory_space=pltpu.SMEM)
HBM = pl.BlockSpec(memory_space=pltpu.HBM)
LABELS = 8


def kernel_call(body, outs, in_specs, scratch=(), flops=0, data=0, out_specs=None, spare=4):
    def call(*args):
        held = [*args, *jax.tree.leaves(outs), *(s for s in scratch if len(s.shape) > 1)]
        places = out_specs or jax.tree.map(lambda _: VMEM, outs)
        room = sum(math.prod(a.shape) * jnp.dtype(a.dtype).itemsize for a in held)
        return pl.pallas_call(
            body,
            out_shape=outs,
            in_specs=in_specs,
            out_specs=places,
            scratch_shapes=list(scratch),
            cost_estimate=pl.CostEstimate(flops=flops, bytes_accessed=data, transcendentals=0),
            compiler_params=pltpu.CompilerParams(vmem_limit_bytes=room + room // 4 + (spare << 20)),
        )(*args)

    return call


def sinc(x):
    angle = x * jnp.float32(jnp.pi)
    safe = jnp.where(x == 0.0, 1.0, angle)
    return jnp.where(x == 0.0, 1.0, jnp.sin(safe) / safe)


def iota(shape, dim):
    return lax.broadcasted_iota(I32, shape, dim)


def warp_body(patches, visits, cap, *refs):
    sources, parcels, held = refs[:5], refs[5:-9], refs[-9:]
    routes, offsets, entries, table, raw, small, large, seats, labels = held
    copies = [
        pltpu.make_async_copy(source, target, small.at[n])
        for n, (source, target) in enumerate(zip(sources[:4], held[:4]))
    ]
    groups = large.shape[0]
    per_group = raw.shape[1] // groups
    loads = [
        pltpu.make_async_copy(
            sources[4].at[:, g * per_group : (g + 1) * per_group],
            raw.at[:, g * per_group : (g + 1) * per_group],
            large.at[g],
        )
        for g in range(groups)
    ]
    for copy in copies + loads:
        copy.start()
    visit_count, tile_cols, side, _ = raw.shape
    tiles = visit_count * tile_cols
    part = side // visits
    sky, visit = lax.axis_index("sky"), lax.axis_index("visit")
    for copy in copies:
        copy.wait()
    row = iota((2 * tiles, side), 0)
    shift = jnp.zeros((2 * tiles, side), F32)
    for n in range(tiles):
        v, i = divmod(n, tile_cols)
        entry = entries[v, i]
        for axis in range(2):
            amount = offsets[v, axis, i].astype(F32) + table[axis, entry]
            shift = jnp.where(row == 2 * n + axis, amount, shift)
    lane = iota((2 * tiles, side), 1)
    step = jnp.where(lane < side // 2, lane, lane - side)
    x = jnp.where(row % 2 == 0, -step, step).astype(F32) - shift
    taps = jnp.where(jnp.abs(x) < 3.0, sinc(x) * sinc(x / 3.0), 0.0)
    near = jnp.abs(iota((side, side), 1) - iota((side, side), 0)) < side // 2

    def spread(index):
        rows = jnp.broadcast_to(taps[index : index + 1, :], (side, side))
        rolled = pltpu.roll(rows, 0, 1, stride=1, stride_axis=0)
        return jnp.where(near, rolled, 0.0).astype(BF)

    for load in loads:
        load.wait()
    for k in range(patches):
        labels[k] = jnp.full((LABELS, side), -1.0, F32)
    count = [jnp.int32(0)] * patches
    for i, v in itertools.product(range(tile_cols), range(visit_count)):
        n = v * tile_cols + i
        halfway = jnp.dot(spread(2 * n), raw[v, i], preferred_element_type=F32).astype(BF)
        warped = jnp.dot(halfway, spread(2 * n + 1), preferred_element_type=F32).astype(BF)
        route = routes[v, i]
        owner = lax.div(route, tile_cols)
        slot = route - owner * tile_cols
        relative = lax.rem(owner - sky + patches, patches)
        seat = sum(jnp.where(relative == k, count[k], 0) for k in range(patches))
        count = [count[k] + (relative == k).astype(I32) for k in range(patches)]
        seats[relative * cap + seat] = warped
        labels[relative, pl.ds(seat, 1), :] = jnp.full(
            (1, side), ((visit * visit_count + v) * tile_cols + slot).astype(F32), F32
        )
    for k in range(patches):
        for r in range(visits):
            parcel = parcels[k * visits + r]
            target = lax.rem(visit + r, visits)
            rows = pl.ds(pl.multiple_of(target * part, part), part)
            for seat in range(cap):
                parcel[seat * part : (seat + 1) * part, :] = seats[k * cap + seat, rows, :]
            parcel[cap * part :, :] = labels[k].astype(BF)


def warp_tiles(patches, visits, cap, raw, offsets, entries, table, routes):
    visit_count, tile_cols, side, _ = raw.shape
    parcel = jax.ShapeDtypeStruct((cap * (side // visits) + LABELS, side), BF)
    small = [routes, jnp.transpose(offsets, (0, 2, 1)), entries, table.T]
    return kernel_call(
        functools.partial(warp_body, patches, visits, cap),
        [parcel] * (patches * visits),
        [HBM] * 5,
        [pltpu.SMEM(a.shape, a.dtype) for a in small]
        + [
            pltpu.VMEM(raw.shape, BF),
            pltpu.SemaphoreType.DMA((len(small),)),
            pltpu.SemaphoreType.DMA((math.gcd(4, tile_cols),)),
            pltpu.VMEM((patches * cap, side, side), BF),
            pltpu.VMEM((patches, LABELS, side), F32),
        ],
        flops=4 * visit_count * tile_cols * side**3,
        data=4 * raw.size,
    )(*(pltpu.with_memory_space_constraint(a, pltpu.HBM) for a in (*small, raw)))


def tables_body(side, block, choice, coefs, listed, taps, heads, tails, plane, bands, mixes, ends):
    for j, t, b in itertools.product(*map(range, (*choice.shape, coefs.shape[0]))):
        row = (j * choice.shape[1] + t) * coefs.shape[0] + b
        mixes[row : row + 1, :] = jnp.full((1, side), coefs[b, choice[j, t]], F32)
    visit_total, tile_cols, per = listed.shape
    width = visit_total * per
    bad = jnp.concatenate([listed[v] for v in range(visit_total)], axis=1)
    bad_row = lax.div(bad, side)
    bad_col = bad - bad_row * side
    place = iota((side, width), 0)
    weight = (lax.div(iota((side, width), 1), per) + 1).astype(F32)
    for t in range(tile_cols):
        rows = jnp.where(bad_row[t : t + 1, :] == place, 1.0, 0.0).astype(BF)
        cols = jnp.where(bad_col[t : t + 1, :] == place, weight, 0.0).astype(BF)
        plane[:, t * side : (t + 1) * side] = lax.dot_general(
            rows, cols, (((1,), (1,)), ((), ())), preferred_element_type=F32
        )
    bases, pairs, lanes = taps.shape
    for b in range(bases):
        for j in range(pairs):
            rows = jnp.broadcast_to(taps[b, j : j + 1, :], (block, lanes))
            bands[b * block : (b + 1) * block, j * lanes : (j + 1) * lanes] = pltpu.roll(
                rows, 0, 1, stride=1, stride_axis=0
            ).astype(BF)
    margin = block // 2
    row, place = iota((block, lanes), 0), lax.rem(iota((block, lanes), 1), margin)
    for n, (source, shift, fits) in enumerate(
        ((heads, 0, place >= row), (tails, lanes - 2 * margin + 1, place <= row - margin))
    ):
        for b, j in itertools.product(range(bases), range(source.shape[1])):
            rows = jnp.broadcast_to(source[b, j : j + 1, :], (block, lanes))
            rolled = pltpu.roll(rows, shift, 1, stride=1, stride_axis=0)
            ends[n, b * block : (b + 1) * block, j * lanes : (j + 1) * lanes] = jnp.where(
                fits, rolled, 0.0
            ).astype(BF)


def make_tables(choice, coefs, listed, kernels, side, block):
    visit_total, tile_cols, per = listed.shape
    bases, taps, _ = kernels.shape
    window = block + taps - 1
    group = max(1, 128 // window)
    padded = -(-taps // group) * group
    turned = jnp.transpose(kernels, (0, 2, 1)).astype(F32)
    columns = jnp.pad(turned, ((0, 0), (0, padded - taps), (0, window - taps))).reshape(
        bases, padded // group, group * window
    )
    margin, lanes = taps // 2, group * window
    groups = -(-taps * margin // lanes)
    fill = ((0, 0), (0, groups * lanes // margin - taps), (0, 0))
    heads, tails = (
        jnp.pad(part, fill).reshape(bases, groups, lanes)
        for part in (turned[:, :, :margin], turned[:, :, margin + 1 :])
    )
    return kernel_call(
        functools.partial(tables_body, side, block),
        [
            jax.ShapeDtypeStruct((side, tile_cols * side), F32),
            jax.ShapeDtypeStruct((bases * block, padded * window), BF),
            jax.ShapeDtypeStruct((choice.size * bases, side), F32),
            jax.ShapeDtypeStruct((2, bases * block, groups * lanes), BF),
        ],
        [SMEM] * 2 + [VMEM] * 4,
        flops=2 * tile_cols * side * side * visit_total * per,
        data=4 * side * side * tile_cols,
    )(choice, coefs.T, listed, columns, heads, tails)


def place(parcels, cap, part, image, of):
    side = parcels[0].shape[1]
    tile_cols, dummy = image.shape[2] // side, image.shape[0] - 1
    for parcel in parcels:
        labels = parcel[cap * part :, :].astype(F32)
        for seat in range(cap):
            label = labels[seat, 0].astype(I32)
            number = lax.div(jnp.maximum(label, 0), tile_cols)
            column = jnp.where(label < 0, 0, label - number * tile_cols) * side
            which = jnp.where(label < 0, dummy, of(number))
            image[which, :, pl.ds(pl.multiple_of(column, side), side)] = parcel[
                seat * part : (seat + 1) * part, :
            ]


def land_body(visits, bands, visit_count, cap, plane, *refs):
    parcels, (slab, partial, image) = refs[:-3], refs[-3:]
    part = slab.shape[1]
    held = visits * visit_count
    visit, band = lax.axis_index("visit"), lax.axis_index("band")
    place(parcels, cap, part, image, lambda number: number)
    rows = pl.ds(pl.multiple_of(visit * part, part), part)
    side = parcels[0].shape[1]
    for start in range(0, image.shape[2], side):
        cols = slice(start, start + side)
        mine = plane[rows, cols]
        total = jnp.zeros(mine.shape, F32)
        high = jnp.full(mine.shape, -jnp.inf, F32)
        low = jnp.full(mine.shape, jnp.inf, F32)
        for n in range(held):
            own, local = divmod(n, visit_count)
            number = ((own * bands + band) * visit_count + local + 1).astype(F32)
            value = image[n, :, cols].astype(F32)
            bad = mine == number
            total = total + jnp.where(bad, 0.0, value)
            high = jnp.maximum(high, jnp.where(bad, -jnp.inf, value))
            low = jnp.minimum(low, jnp.where(bad, jnp.inf, value))
        partial[0, :, cols] = total.astype(BF)
        partial[1, :, cols] = high.astype(BF)
        partial[2, :, cols] = low.astype(BF)
    for j in range(visit_count):
        slab[j] = image[visit * visit_count + j]


def land_tiles(visits, bands, visit_count, cap, tile_cols, plane, parcels):
    side = parcels[0].shape[1]
    part = (parcels[0].shape[0] - LABELS) // cap
    width = tile_cols * side
    return kernel_call(
        functools.partial(land_body, visits, bands, visit_count, cap),
        [
            jax.ShapeDtypeStruct((visit_count, part, width), BF),
            jax.ShapeDtypeStruct((3, part, width), BF),
        ],
        [VMEM] * (1 + len(parcels)),
        [pltpu.VMEM((visits * visit_count + 1, part, width), BF)],
        flops=10 * visits * visit_count * part * width,
        data=4 * visits * visit_count * part * width,
    )(plane, *parcels)


def coadd_body(visit_total, margin, plane, *refs):
    partials, (coadd, share, edge) = refs[:-3], refs[-3:]
    part, some = coadd.shape[0], share.shape[0]
    visit, band = lax.axis_index("visit"), lax.axis_index("band")
    rows = pl.ds(pl.multiple_of(visit * part, part), part)
    width = coadd.shape[1]
    step = math.gcd(128, width)
    for first in range(0, width, step):
        cols = slice(first, first + step)
        total, high, low = (partials[0][n, :, cols].astype(F32) for n in range(3))
        for other in partials[1:]:
            total = total + other[0, :, cols].astype(F32)
            high = jnp.maximum(high, other[1, :, cols].astype(F32))
            low = jnp.minimum(low, other[2, :, cols].astype(F32))
        scale = jnp.where(
            plane[rows, cols] > 0.0, 1.0 / (visit_total - 3.0), 1.0 / (visit_total - 2.0)
        )
        coadd[:, cols] = ((total - high - low) * scale).astype(BF)
    share[...] = coadd[pl.ds(pl.multiple_of(band * some, some), some), :]
    start = pl.multiple_of(jnp.where(visit == 0, 0, part - margin), margin)
    edge[...] = coadd[pl.ds(start, margin), :]


def shifted(image, rows, margin, taps, side, first, until, made):
    width, height = image.shape[1], rows.stop - rows.start
    lane = iota((height, side), 1)
    blank = jnp.zeros((height, side), BF)
    shifts = []
    for dx in range(taps):
        shift = dx - margin
        low, high = (first - 1, until) if shift < 0 else (first, until + 1)
        for t in range(low, high) if shift else ():
            if not 0 <= t < width // side:
                made[t, dx] = blank
            elif (t, dx) not in made:
                made[t, dx] = pltpu.roll(image[rows, t * side : (t + 1) * side], -shift % side, 1)
        tiles = []
        for t in range(first, until):
            if shift < 0:
                tiles.append(jnp.where(lane < -shift, made[t - 1, dx], made[t, dx]))
            elif shift > 0:
                tiles.append(jnp.where(lane < side - shift, made[t, dx], made[t + 1, dx]))
            else:
                tiles.append(image[rows, t * side : (t + 1) * side])
        shifts.append(jnp.concatenate(tiles, axis=1))
    return shifts


def apply_rows(left, shifts, pick):
    right = jnp.concatenate([pick(dx, each) for dx, each in enumerate(shifts)], axis=0)
    return jnp.dot(left, right, preferred_element_type=F32)


def collect_body(visits, visit_count, cap, *refs):
    count = len(refs) - (visits - 1)
    parcels, others = refs[:count], refs[count:]
    each = count // (visits - 1)
    part = others[0].shape[1]
    for r, other in enumerate(others):
        place(
            parcels[r * each : (r + 1) * each],
            cap,
            part,
            other,
            lambda number: lax.rem(number, visit_count),
        )


def filter_ahead_body(margin, taps, side, per, low, bands, own, sums, edge):
    part, width = own.shape
    window = 2 * margin + taps - 1
    left = bands[:, : taps * window]
    rows = slice(0, window - margin) if low else slice(part - window + margin, part)
    outer = slice(0, margin) if low else slice(window - 2 * margin, window - margin)
    blank = jnp.zeros((margin, per * side), BF)
    made = {}
    for t in range(0, width // side, per):
        cols = slice(t * side, (t + per) * side)
        shifts = shifted(own, rows, margin, taps, side, t, t + per, made)
        sums[:, cols] = apply_rows(
            left, shifts, lambda dx, x: jnp.concatenate([blank, x] if low else [x, blank])
        )
        for dx, x in enumerate(shifts):
            edge[dx, :, cols] = x[outer]


def joined(pieces, halos, place_piece):
    sky, visit, band = (lax.axis_index(name) for name in ("sky", "visit", "band"))
    patches, visits = lax.axis_size("sky"), lax.axis_size("visit")
    for n, piece in enumerate(pieces):
        some = piece.shape[0]
        place_piece(lax.rem(visit + 1 + n // 2, visits), lax.rem(band + n, 2) * some, piece[...])
    mine = lax.rem(visit, 2) == band
    below = jnp.where(mine, halos[0][...], halos[1][...])
    above = jnp.where(mine, halos[1][...], halos[0][...])
    below = jnp.where(sky == patches - 1, jnp.zeros_like(below), below)
    above = jnp.where(sky == 0, jnp.zeros_like(above), above)
    return above, below


def render_body(
    margin, taps, tile_cols, per, bands, ends, mixes, plane, low, high, head, tail, slab, others, *refs
):
    width = plane.shape[1]
    pieces, halos, (out, result, sems, image) = refs[:-6], refs[-6:-4], refs[-4:]
    block, step = 2 * margin, per * (width // tile_cols)
    part = 2 * block
    window = block + taps - 1
    visit_count, side = result.shape[0], width // tile_cols
    bases = bands.shape[0] // block
    visit, band = lax.axis_index("visit"), lax.axis_index("band")
    band_count = lax.axis_size("band")
    first = visit == 0

    def put(_, start, piece):
        rows = pl.ds(pl.multiple_of(start, margin), piece.shape[0])
        image[rows, :] = piece

    above, below = joined(pieces, halos, put)
    image[part : part + margin, :] = above
    image[part + margin :, :] = below
    over, under = slice(part, part + margin), slice(part + margin, part + 2 * margin)
    top, bottom = slice(0, margin), slice(part - margin, part)
    numbers = [
        ((visit * band_count + band) * visit_count + j + 1).astype(F32)
        for j in range(visit_count)
    ]
    left = bands[:, : taps * window]

    def finish(start, n, c, source, value):
        value = value.astype(BF).astype(F32)
        rows = pl.ds(pl.multiple_of(start + n * block, block), block)
        for t in range(c * step // side, (c + 1) * step // side):
            cols = slice(t * side, (t + 1) * side)
            inset = slice(t * side - c * step, (t + 1) * side - c * step)
            planes = [value[b * block : (b + 1) * block, inset] for b in range(bases)]
            bad = plane[rows, cols]
            for j in range(visit_count):
                row = (j * tile_cols + t) * bases
                template = sum(mixes[row + b : row + b + 1, :] * planes[b] for b in range(bases))
                pixels = source[j, n * block : (n + 1) * block, cols].astype(F32) - template
                result[j, rows, cols] = jnp.where(bad == numbers[j], 0.0, pixels).astype(BF)

    copies = []
    made = {}
    for c in range(width // step):
        cols = slice(c * step, (c + 1) * step)
        shifts = shifted(image, slice(0, part + 2 * margin), margin, taps, side, c * per, (c + 1) * per, made)

        def upper(dx, x):
            before = jnp.where(first, tail[dx, :, cols], x[over])
            return jnp.concatenate([before, x[: window - margin]])

        def lower(dx, x):
            after = jnp.where(first, x[under], head[dx, :, cols])
            return jnp.concatenate([x[part - window + margin : part], after])

        start = (1 - visit) * part
        finish(start, 0, c, others, apply_rows(left, shifts, upper))
        finish(start, 1, c, others, apply_rows(left, shifts, lower))
        lack = apply_rows(
            ends[0, :, : taps * margin], shifts, lambda dx, x: jnp.where(first, x[over], x[bottom])
        )
        finish(visit * part, 0, c, slab, low[:, cols] + lack)
        lack = apply_rows(
            ends[1, :, : taps * margin], shifts, lambda dx, x: jnp.where(first, x[top], x[under])
        )
        finish(visit * part, 1, c, slab, high[:, cols] + lack)
        copies.append(
            pltpu.make_async_copy(result.at[:, :, cols], out.at[:, :, cols], sems.at[c])
        )
        copies[-1].start()
    for copy in copies:
        copy.wait()


def filter_body(margin, taps, side, per, bands, own, *refs):
    pieces, halos, (out, image) = refs[:-4], refs[-4:-2], refs[-2:]
    part, width = own.shape
    block = 2 * margin
    window = block + taps - 1

    def put(turn, start, piece):
        start = pl.multiple_of(turn * part + start + margin, margin)
        image[pl.ds(start, piece.shape[0])] = piece

    above, below = joined(pieces, halos, put)
    image[:margin] = above
    image[image.shape[0] - margin :] = below
    put(lax.axis_index("visit"), 0, own[...])
    made = {}
    for t in range(0, width // side, per):
        shifts = shifted(image, slice(0, image.shape[0]), margin, taps, side, t, t + per, made)
        for n in range(out.shape[0]):
            rows = slice(n * block, n * block + window)
            value = apply_rows(bands[:, : taps * window], shifts, lambda dx, x: x[rows])
            out[n, :, t * side : (t + per) * side] = value.astype(BF)


def finish_body(visits, bands, tile_cols, mixes, filtered, plane, *refs):
    slabs, (out, image, result, sems) = refs[:-4], refs[-4:]
    visit, band = lax.axis_index("visit"), lax.axis_index("band")
    part, width = slabs[0].shape[1:]
    visit_count = image.shape[0]
    blocks = filtered.shape[0]
    bases = mixes.shape[0] // (visit_count * tile_cols)
    block = filtered.shape[1] // bases
    side = width // tile_cols
    for r in range(visits):
        start = pl.multiple_of(lax.rem(visit + r, visits) * part, part)
        for j in range(visit_count):
            image[j, pl.ds(start, part), :] = slabs[r][j]
    numbers = [
        ((visit * bands + band) * visit_count + j + 1).astype(F32) for j in range(visit_count)
    ]
    copies = []
    for n in range(blocks):
        rows = slice(n * block, (n + 1) * block)
        for t in range(tile_cols):
            cols = slice(t * side, (t + 1) * side)
            planes = [
                filtered[n, b * block : (b + 1) * block, cols].astype(F32) for b in range(bases)
            ]
            bad = plane[rows, cols]
            for j in range(visit_count):
                row = (j * tile_cols + t) * bases
                template = sum(mixes[row + b : row + b + 1, :] * planes[b] for b in range(bases))
                value = image[j, rows, cols].astype(F32) - template
                result[j, rows, cols] = jnp.where(bad == numbers[j], 0.0, value).astype(BF)
        copies.append(pltpu.make_async_copy(result.at[:, rows], out.at[:, rows], sems.at[n]))
        copies[-1].start()
    for copy in copies:
        copy.wait()


def on_device(
    raw_tiles,
    pixel_offsets,
    shift_entry_index,
    shift_table,
    tile_routes,
    bad_pixels,
    basis_kernels,
    basis_choice,
    coef_table,
):
    visit_count, tile_cols, side = raw_tiles.shape[:3]
    patches, visits, bands = (lax.axis_size(name) for name in ("sky", "visit", "band"))
    cap = (visit_count * tile_cols + patches - 1) // patches + 1
    part, width = side // visits, tile_cols * side
    visit_total = bad_pixels.shape[0]
    bases, taps = basis_kernels.shape[:2]
    margin = taps // 2
    block = 2 * margin

    parcels = warp_tiles(
        patches, visits, cap, raw_tiles, pixel_offsets, shift_entry_index, shift_table, tile_routes
    )
    far = sorted(range(patches), key=lambda k: (-min(k, patches - k), -k))
    order = [k * visits + r for r in reversed(range(visits)) for k in far if k + r > 0]
    arrived = {0: parcels[0]}
    for n in order:
        k, r = divmod(n, visits)
        pairs = [
            (s * visits + v, (s + k) % patches * visits + (v + r) % visits)
            for s in range(patches)
            for v in range(visits)
        ]
        arrived[n] = lax.ppermute(parcels[n], ("sky", "visit"), pairs)
    own_others = []
    for r in range(1, visits):
        own_others.append(parcels[r])
        for k in (k for k in far if k > 0):
            own_others.append(
                lax.ppermute(
                    arrived[k * visits + r], "visit", [(v, (v - r) % visits) for v in range(visits)]
                )
            )
    plane, toeplitz, mixes, ends = make_tables(
        basis_choice, coef_table, bad_pixels, basis_kernels, side, block
    )
    slab, partial = land_tiles(
        visits, bands, visit_count, cap, tile_cols, plane, list(arrived.values())
    )

    partials = [partial] + [
        lax.ppermute(partial, "band", [(b, (b + q) % bands) for b in range(bands)])
        for q in range(1, bands)
    ]
    coadd, share, edge = kernel_call(
        functools.partial(coadd_body, visit_total, margin),
        [jax.ShapeDtypeStruct((rows, width), BF) for rows in (part, part // bands, margin)],
        [VMEM] * (1 + bands),
        flops=8 * part * width,
        data=8 * part * width,
    )(plane, *partials)

    def turn(r):
        return [(v, (v - r) % visits) for v in range(visits)]

    swap = [(b, (b + 1) % bands) for b in range(bands)]
    pieces = []
    for r in range(1, visits):
        pieces.append(lax.ppermute(share, "visit", turn(r)))
        pieces.append(lax.ppermute(pieces[-1], "band", swap))
    halos = []
    for first in range(0, visits, bands):
        pairs = []
        for s, b in itertools.product(range(patches), range(bands)):
            r = first + b
            top = ((s - 1) % patches, r)
            bottom = ((s + 1) % patches, visits - 1 - r)
            for v, (to_s, to_v) in ((0, top), (visits - 1, bottom)):
                pairs.append(((s * visits + v) * bands + b, (to_s * visits + to_v) * bands + b))
        halos.append(lax.ppermute(edge, ("sky", "visit", "band"), pairs))
    halo = functools.reduce(jnp.add, halos)
    halos = [halo, lax.ppermute(halo, "band", swap)]
    others = kernel_call(
        functools.partial(collect_body, visits, visit_count, cap),
        [jax.ShapeDtypeStruct((visit_count + 1, part, width), BF)] * (visits - 1),
        [VMEM] * len(own_others),
        flops=part * width,
        data=4 * visit_count * side * width,
    )(*own_others)
    work = 2 * bases * side * width * taps * (block + taps - 1)
    per = math.gcd(4, tile_cols)
    result = jax.ShapeDtypeStruct((visit_count, side, width), BF)
    if visits == 2 and part == 2 * block:
        sums, edges = [], []
        for low in (True, False):
            one, edge = kernel_call(
                functools.partial(filter_ahead_body, margin, taps, side, per, low),
                [
                    jax.ShapeDtypeStruct((bases * block, width), F32),
                    jax.ShapeDtypeStruct((taps, margin, width), BF),
                ],
                [VMEM] * 2,
                flops=work // 4,
                data=4 * bases * part * width,
                spare=16,
            )(toeplitz, coadd)
            sums.append(one)
            edges.append(edge)
        return kernel_call(
            functools.partial(render_body, margin, taps, tile_cols, per),
            result,
            [VMEM] * (10 + len(pieces) + 2),
            [
                pltpu.VMEM(result.shape, BF),
                pltpu.SemaphoreType.DMA((tile_cols // per,)),
                pltpu.VMEM((part + 2 * margin, width), BF),
            ],
            flops=work // 2,
            data=2 * bases * side * width,
            spare=24,
            out_specs=HBM,
        )(toeplitz, ends, mixes, plane, *sums, *edges, slab, *others, *pieces, *halos)
    filtered = kernel_call(
        functools.partial(filter_body, margin, taps, side, per),
        jax.ShapeDtypeStruct((side // block, bases * block, width), BF),
        [VMEM] * (2 + len(pieces) + 2),
        [pltpu.VMEM((side + 2 * margin, width), BF)],
        flops=work,
        data=2 * bases * side * width,
        spare=24,
    )(toeplitz, coadd, *pieces, *halos)
    return kernel_call(
        functools.partial(finish_body, visits, bands, tile_cols),
        result,
        [VMEM] * (3 + visits),
        [
            pltpu.VMEM(result.shape, BF),
            pltpu.VMEM(result.shape, BF),
            pltpu.SemaphoreType.DMA((side // block,)),
        ],
        flops=20 * visit_count * side * width,
        data=4 * visit_count * side * width,
        out_specs=HBM,
    )(mixes, filtered, plane, slab, *others)


def solution(mesh):
    return jax.shard_map(
        on_device,
        mesh=mesh,
        in_specs=(
            P(("group", "visit", "band"), "sky", None, None),
            P(("group", "visit", "band"), "sky", None),
            P(("group", "visit", "band"), "sky"),
            P(),
            P(("group", "visit", "band"), "sky"),
            P("group", "sky", None),
            P(),
            P(("group", "visit", "band"), "sky"),
            P(),
        ),
        out_specs=P(("group", "visit", "band"), "sky", None),
        check_vma=False,
    )
```
